256 devices in a mesh: ctx: 8 (over y, core), exp: 32 (over z, x).
Axes of the slice: x: 4, y: 4, z: 8, core: 2. Of those that a mesh axis runs over, the one named last changes fastest.
Arguments:
- hits: bfloat16 [32768, 2048], P(('ctx', 'exp')), may hold values from -6 to 6
- cotangent: bfloat16 [32768, 2048], P(('ctx', 'exp')), may hold values from -6 to 6
- combine: float32 [32768, 2], P(('ctx', 'exp')), may hold values from 0.1 to 1
- expert_ids: int32 [32768, 2], P(('ctx', 'exp')), may hold values from 0 to 31, all different within a row; in each aligned block of 128 rows (0 to 127, 128 to 255, ...) at most 12 rows name the same one
- gate_weight: bfloat16 [32, 2048, 768], P('exp'), may hold values from -0.125 to 0.125
- up_weight: bfloat16 [32, 2048, 768], P('exp'), may hold values from -0.125 to 0.125
- down_weight: bfloat16 [32, 2048, 768], P('exp'), may hold values from -0.21875 to 0.21875
Outputs:
- mixed: bfloat16 [32768, 2048], P(('ctx', 'exp'))
- input_grads: bfloat16 [32768, 2048], P(('ctx', 'exp'))
- combine_grads: float32 [32768, 2], P(('ctx', 'exp'))
- gate_grads: bfloat16 [32, 2048, 768], P('exp', 'ctx')
- up_grads: bfloat16 [32, 2048, 768], P('exp', 'ctx')
- down_grads: bfloat16 [32, 2048, 768], P('exp', 'ctx')
The draws below stay inside these ranges and needn't reach their ends.
Inputs may be any that keep to these rules, and one draw needn't show every extreme that they name: `expert_ids`: the two ids of a hit differ. Among the 128 hits of one device no expert is named more than 12 times, and in every draw some device names some expert exactly 12 times.
All inputs are finite; a program needn't handle non-finite values.
Results may differ from the reference program's by a relative error of at most 0.017.
Values may be sent and summed in bfloat16 or wider, within the bound.
A program may use at most 128 MiB of HBM per device.

```python
import math
import jax
import jax.numpy as jnp
import numpy as np
from jax import lax

D = 2048
FF = 768
TOK_DEV = 128
EXPERTS = 32
CAP = 12
TOKENS = 32768
N_CTX = 8
N_EXP = 32


def levels(rng, extent, cuts, least, top_value):
    gain, own = 1.0, jax.random.fold_in(rng, 6)
    for dim, shards_of in cuts:
        heights = jnp.exp(jax.random.uniform(jax.random.fold_in(own, dim), (shards_of,), jnp.float32, least / len(cuts), top_value / len(cuts)))
        gain = gain * jnp.repeat(heights, extent[dim] // shards_of).reshape([-1 if axis == dim else 1 for axis in range(len(extent))])
    return gain


def routed_block(rng, own, number, rows, amount, top, most, slope):
    sequence = jax.random.permutation(rng, amount)
    heavy_load, common = shares(amount, rows * top, most, slope, True), shares(amount, rows * top, most, slope, False)
    places = jnp.arange(amount)

    def named(lengths, offset_by):
        used = int((lengths > 0).sum())
        fixed = max(1, used // 4)
        moved = fixed + (places - fixed + offset_by * (used - fixed)) % max(1, amount - fixed)
        return jnp.zeros((amount,), jnp.int32).at[sequence[jnp.where(places < fixed, places, moved)]].set(jnp.asarray(lengths, jnp.int32))

    lengths = jnp.where(number % 4 == 0, named(heavy_load, number // 4), named(common, number - number // 4 - 1))
    mixed = jax.random.permutation(jax.random.fold_in(own, 3), amount)
    donor, taker = mixed[0:amount // 2 * 2:2], mixed[1:amount // 2 * 2:2]
    slack = jnp.minimum(lengths[donor] - 1, most - lengths[taker]) // 2
    slack = jnp.where((donor == sequence[0]) | (taker == sequence[0]) | (lengths[taker] == 0), 0, jnp.maximum(slack, 0))
    moved = jax.random.randint(jax.random.fold_in(own, 4), (amount // 2,), 0, 1 << 20) % (slack + 1)
    lengths = lengths.at[donor].add(-moved).at[taker].add(moved)
    items = jnp.searchsorted(jnp.cumsum(lengths), jnp.arange(rows * top), side="right").astype(jnp.int32)
    table = items.reshape(top, rows).T
    table = table[jax.random.permutation(jax.random.fold_in(own, 1), rows)]
    offset_by = jax.random.randint(jax.random.fold_in(own, 2), (rows, 1), 0, top)
    return jnp.take_along_axis(table, (jnp.arange(top)[None, :] + offset_by) % top, axis=1)


def shares(number_of, total, limit, slope, full):
    loads = [(1 << 20) // math.isqrt(rank ** slope) + 1 for rank in range(1, number_of + 1)]
    largest = limit if full else min(limit, max(-(-total // number_of), total * loads[0] // sum(loads)))
    least = 1 if total - largest >= number_of - 1 else 0
    given, surplus = [largest] + [least] * (number_of - 1), total - largest - least * (number_of - 1)
    while surplus > 0:
        movable = [i for i in range(1, number_of) if given[i] < largest] or [i for i in range(1, number_of) if given[i] < limit]
        pool, left = sum([loads[i] for i in movable]), surplus
        for i in movable:
            addition = min(limit - given[i], max(1, left * loads[i] // pool), surplus)
            given[i] = given[i] + addition
            surplus = surplus - addition
    return np.array(given)


def gaussian(key, dims, deviation, limit, split=(), kind=jnp.bfloat16):
    values = jax.random.normal(key, dims, jnp.float32) * deviation
    if len(split) > 0:
        values = levels(key, dims, split, -0.22, 0.18) * values
    return jnp.clip(values, min=-limit, max=limit).astype(kind)


def setup_inputs(seed: int = 0) -> dict:
    arg_keys = jax.random.split(jax.random.key(seed), 8)
    hits = gaussian(arg_keys[0], (TOKENS, D), 1.0, 6.0, ((0, 256),))
    cotangent = gaussian(arg_keys[1], (TOKENS, D), 1.0, 6.0, ((0, 256),))
    combine = jnp.clip(0.1 + 0.9 * jax.random.uniform(arg_keys[2], (TOKENS, 2), jnp.float32) ** levels(arg_keys[2], (TOKENS, 2), ((0, 256),), -0.2, 0.2), 0.1, 1.0)
    expert_ids_keys = jax.random.split(jax.random.fold_in(arg_keys[3], 1), TOKENS // TOK_DEV)
    expert_ids_turns = jax.random.permutation(jax.random.fold_in(arg_keys[3], 3), TOKENS // TOK_DEV)
    expert_ids = jax.vmap(lambda own, number: routed_block(jax.random.fold_in(arg_keys[3], 2), own, number, TOK_DEV, EXPERTS, 2, CAP, 2))(expert_ids_keys, expert_ids_turns).reshape((TOKENS, 2))
    gate_weight = gaussian(arg_keys[4], (EXPERTS, D, FF), D ** -0.5, 0.125, ((0, 32),))
    up_weight = gaussian(arg_keys[5], (EXPERTS, D, FF), D ** -0.5, 0.125, ((0, 32),))
    down_weight = gaussian(arg_keys[6], (EXPERTS, D, FF), FF ** -0.5, 0.21875, ((0, 32),))
    return {"hits": hits, "cotangent": cotangent, "combine": combine, "expert_ids": expert_ids, "gate_weight": gate_weight, "up_weight": up_weight, "down_weight": down_weight}


grad_scale = 0.0625


def expert_pass(slot_hits, slot_cot, w_gate, w_up, w_down):
    contract_hidden = (((1,), (1,)), ((), ()))
    gate_value = jnp.dot(slot_hits, w_gate, preferred_element_type=jnp.float32)
    up_value = jnp.dot(slot_hits, w_up, preferred_element_type=jnp.float32)
    sigmoid_gate = jax.nn.sigmoid(gate_value)
    active = gate_value * sigmoid_gate
    hidden = (active * up_value).astype(jnp.bfloat16)
    outputs = lax.dot_general(hidden, w_down, contract_hidden, preferred_element_type=jnp.float32).astype(jnp.bfloat16)
    grad_hidden = jnp.dot(slot_cot, w_down, preferred_element_type=jnp.float32)
    grad_up = (grad_hidden * active).astype(jnp.bfloat16)
    grad_gate = (grad_hidden * up_value * sigmoid_gate * (1.0 + gate_value * (1.0 - sigmoid_gate))).astype(jnp.bfloat16)
    grad_input = lax.dot_general(grad_gate, w_gate, contract_hidden, preferred_element_type=jnp.float32)
    grad_input = grad_input + lax.dot_general(grad_up, w_up, contract_hidden, preferred_element_type=jnp.float32)
    return outputs, grad_input.astype(jnp.bfloat16), hidden, grad_gate, grad_up


def ctx_partials(left_rows, right_rows):
    left_block = left_rows.reshape(N_CTX, -1, left_rows.shape[1]).astype(jnp.float32)
    right_block = right_rows.reshape(N_CTX, -1, right_rows.shape[1]).astype(jnp.float32)
    block_terms = jnp.einsum("crd,crf->cdf", left_block, right_block)
    rounded = lax.optimization_barrier(block_terms.astype(jnp.bfloat16))
    summed = jnp.sum(rounded.astype(jnp.float32), axis=0)
    return (summed * grad_scale).astype(jnp.bfloat16)


def reference(hits, cotangent, combine, expert_ids, gate_weight, up_weight, down_weight):
    devices_all = N_CTX * N_EXP
    routed = expert_ids.reshape(devices_all, 2 * TOK_DEV)
    catalog = jnp.arange(EXPERTS, dtype=jnp.int32)
    one_hot = (routed[:, :, None] == catalog[None, None, :]).astype(jnp.int32)
    slot_rank = jnp.sum((jnp.cumsum(one_hot, axis=1) - one_hot) * one_hot, axis=2)
    device_index = jnp.arange(devices_all, dtype=jnp.int32)[:, None]
    position = routed * (devices_all * CAP) + device_index * CAP + slot_rank
    pair_count = 2 * TOKENS
    table = jnp.full((EXPERTS * devices_all * CAP,), pair_count, jnp.int32)
    table = table.at[position.reshape(-1)].set(jnp.arange(pair_count, dtype=jnp.int32))
    table = table.reshape(EXPERTS, devices_all * CAP)
    flat_combine = combine.reshape(-1)

    def per_expert(carry, inputs):
        out_pairs, grad_pairs = carry
        w_gate, w_up, w_down, pair_ids = inputs
        valid = pair_ids < pair_count
        safe_pairs = jnp.where(valid, pair_ids, 0).astype(jnp.int32)
        owners = safe_pairs // 2
        slot_hits = jnp.where(valid[:, None], hits[owners], jnp.zeros((), jnp.bfloat16))
        weights_here = jnp.where(valid, flat_combine[safe_pairs], jnp.zeros((), jnp.float32))
        slot_cot = (weights_here[:, None] * cotangent[owners].astype(jnp.float32)).astype(jnp.bfloat16)
        outputs, grad_input, hidden, grad_gate, grad_up = expert_pass(slot_hits, slot_cot, w_gate, w_up, w_down)
        out_pairs = out_pairs.at[pair_ids].set(outputs, mode="drop")
        grad_pairs = grad_pairs.at[pair_ids].set(grad_input, mode="drop")
        gate_part = ctx_partials(slot_hits, grad_gate)
        up_part = ctx_partials(slot_hits, grad_up)
        down_part = ctx_partials(slot_cot, hidden)
        return (out_pairs, grad_pairs), (gate_part, up_part, down_part)

    zero_pairs = jnp.zeros((pair_count, D), jnp.bfloat16)
    (out_pairs, grad_pairs), (gate_grads, up_grads, down_grads) = lax.scan(
        per_expert, (zero_pairs, zero_pairs), (gate_weight, up_weight, down_weight, table))
    expert_out = out_pairs.reshape(TOKENS, 2, D).astype(jnp.float32)
    mixed = jnp.sum(combine[:, :, None] * expert_out, axis=1).astype(jnp.bfloat16)
    combine_grads = jnp.sum(cotangent[:, None, :].astype(jnp.float32) * expert_out, axis=2)
    input_grads = jnp.sum(grad_pairs.reshape(TOKENS, 2, D).astype(jnp.float32), axis=1).astype(jnp.bfloat16)
    return (mixed, input_grads, combine_grads, gate_grads, up_grads, down_grads)
```

```python
import functools

import jax
import jax.numpy as jnp
from jax import lax
from jax.experimental import pallas as pl
from jax.experimental.pallas import tpu as pltpu
from jax.sharding import PartitionSpec as P

MESH = pl.DeviceIdType.MESH
F32 = jnp.float32
BF16 = jnp.bfloat16

grad_scale = 0.0625
NZ, NX, NY = 8, 4, 4
EXPERTS = NZ * NX
CAP = 12
T = 128
D = 2048
FF = 768
RB = 16
Q = 512
W = 3 * Q
ROWS = EXPERTS * RB
CS = D // 8
HALF = CS // 2
DYS = (2, 1, 3, 0)


def shift_order():
    order = []
    for dx in range(NX):
        for dz in (1, 7, 2, 6, 3, 5, 4, 0):
            if (dz, dx) != (0, 0):
                order.append((dz, dx))
    return order


def nn(a, b):
    return jnp.dot(a, b, preferred_element_type=F32)


def nt(a, b):
    return lax.dot_general(a, b, (((1,), (1,)), ((), ())), preferred_element_type=F32)


def tn(a, b):
    return lax.dot_general(a, b, (((0,), (0,)), ((), ())), preferred_element_type=F32)


def iota(shape, dim):
    return lax.broadcasted_iota(jnp.int32, shape, dim)


def bits(cond):
    return jnp.where(cond, 1.0, 0.0).astype(BF16)


def kernel(
    hits, cotangent, combine, expert_ids, wg_hbm, wu_hbm, wd_hbm,
    mixed_out, igrad_out, cgrad_out, gate_out, up_out, down_out,
    wg, wu, wd, send, recv, xs, cs, act, fac, hid, gg, gu,
    po, pr, st, ra, rb, r1, r3,
    w_sem, send_sem, recv_sem, po_sem, pr_sem, y_send, y_recv,
):
    c = lax.axis_index("ctx")
    me = lax.axis_index("exp")
    z, x = me // NX, me % NX
    y, core = c // 2, c % 2
    sibling = y * 2 + 1 - core
    y_next = ((y + 1) % NY) * 2 + core
    y_prev = ((y + NY - 1) % NY) * 2 + core
    order = shift_order()

    def peer(dz, dx):
        return ((z + dz) % NZ) * NX + (x + dx) % NX

    loads = []
    for i, (src, dst) in enumerate(((wg_hbm, wg), (wu_hbm, wu), (wd_hbm, wd))):
        copy = pltpu.make_async_copy(src.at[0], dst, w_sem.at[i])
        copy.start()
        loads.append(copy)

    barrier = pltpu.get_barrier_semaphore()
    for dz, dx in order:
        pl.semaphore_signal(barrier, inc=1, device_id=(c, peer(dz, dx)), device_id_type=MESH)
    for other in (sibling, y_next, y_prev):
        pl.semaphore_signal(barrier, inc=1, device_id=(other, me), device_id_type=MESH)

    lane = iota((T, 128), 1)
    ids = [expert_ids[:, k : k + 1] for k in range(2)]
    named = bits((lane == ids[0]) | (lane == ids[1]))
    earlier = bits(iota((T, T), 1) < iota((T, T), 0))
    before = nn(earlier, named)
    s_col, v_col = [], []
    for k in range(2):
        rank = jnp.sum(jnp.where(lane == ids[k], before, 0.0), axis=1, keepdims=True).astype(jnp.int32)
        block = (((ids[k] >> 2) - z) & (NZ - 1)) * NX + (((ids[k] & (NX - 1)) - x) & (NX - 1))
        s_col.append(block * RB + rank)
        v_col.append((rank >> 2) * ROWS + block * RB + CAP + (rank & 3))
    table = jnp.where(lane == 0, s_col[0], jnp.where(lane == 1, s_col[1], jnp.where(lane == 2, v_col[0], v_col[1])))
    turned = jnp.transpose(table.astype(F32)).astype(jnp.int32)
    s_row = [turned[k : k + 1, :] for k in range(2)]
    v_row = [turned[2 + k : 3 + k, :] for k in range(2)]
    rows_t = iota((ROWS, T), 0)

    def copies(phase, back, src, dst):
        for dz, dx in order:
            i = dz * NX + dx
            to = peer(NZ - dz, NX - dx) if back else peer(dz, dx)
            pltpu.make_async_remote_copy(
                src_ref=src.at[pl.ds(RB * i, RB)],
                dst_ref=dst.at[pl.ds(RB * i, RB)],
                send_sem=send_sem.at[phase],
                recv_sem=recv_sem.at[phase],
                device_id=(c, to),
                device_id_type=MESH,
            ).start()
        dst[0:RB, :] = src[0:RB, :]

    def whole(phase):
        return pltpu.make_async_remote_copy(
            src_ref=send.at[phase, pl.ds(RB, ROWS - RB)],
            dst_ref=recv.at[phase, pl.ds(RB, ROWS - RB)],
            send_sem=send_sem.at[phase],
            recv_sem=recv_sem.at[phase],
            device_id=(c, peer(1, 0)),
            device_id_type=MESH,
        )

    d_any = bits((rows_t == s_row[0]) | (rows_t == s_row[1]))
    for b in range(3):
        t_any = bits((rows_t + ROWS * b == v_row[0]) | (rows_t + ROWS * b == v_row[1]))
        left = jnp.concatenate([d_any, t_any], axis=1)
        right = jnp.concatenate([hits[:, Q * b : Q * b + Q], hits[:, W:]], axis=0)
        send[0, :, Q * b : Q * b + Q] = nn(left, right).astype(BF16)
    pl.semaphore_wait(barrier, len(order) + 3)
    copies(0, False, send.at[0], recv.at[0])

    for b in range(3):
        left, right = [], []
        for k in range(2):
            weight = combine[:, k : k + 1]
            left.append(bits(rows_t == s_row[k]))
            right.append((weight * cotangent[:, Q * b : Q * b + Q].astype(F32)).astype(BF16))
            left.append(bits(rows_t + ROWS * b == v_row[k]))
            right.append((weight * cotangent[:, W:].astype(F32)).astype(BF16))
        send[1, :, Q * b : Q * b + Q] = nn(
            jnp.concatenate(left, axis=1), jnp.concatenate(right, axis=0)
        ).astype(BF16)
    whole(0).wait_send()
    copies(1, False, send.at[1], recv.at[1])

    row = iota((256, 256), 0)
    col = iota((256, 256), 1)
    same = (row >> 4) == (col >> 4)
    keep = jnp.where((iota((256, 1), 0) & 15) < CAP, 1.0, 0.0)
    keep_all = jnp.where((iota((ROWS, 1), 0) & 15) < CAP, 1.0, 0.0)

    def unpack(src, dst):
        for h in range(ROWS // 256):
            part = pl.ds(256 * h, 256)
            tail = jnp.zeros((256, Q), F32)
            for b in range(3):
                block = src[part, Q * b : Q * b + Q]
                dst[part, Q * b : Q * b + Q] = (block.astype(F32) * keep).astype(BF16)
                pick = bits(
                    same & ((row & 15) < CAP) & (((row & 15) >> 2) == b) & ((col & 15) == CAP + (row & 3))
                )
                tail = tail + nn(pick, block)
            dst[part, W:] = tail.astype(BF16)

    def pack(product, dst):
        tail = product(3).astype(BF16)
        for b in range(3):
            main = product(b) * keep_all
            pick = bits(same & ((row & 15) >= CAP) & ((col & 15) == 4 * b + (row & 15) - CAP))
            for h in range(ROWS // 256):
                dst[256 * h : 256 * h + 256, Q * b : Q * b + Q] = (
                    main[256 * h : 256 * h + 256] + nn(pick, tail[256 * h : 256 * h + 256])
                ).astype(BF16)

    whole(0).wait_recv()
    unpack(recv.at[0], xs)
    loads[0].wait()
    loads[1].wait()

    @pl.loop(0, FF // 256)
    def _(n):
        part = pl.ds(pl.multiple_of(n * 256, 256), 256)
        gate = nn(xs[...], wg[:, part])
        up = nn(xs[...], wu[:, part])
        sig = jax.nn.sigmoid(gate)
        active = gate * sig
        act[:, part] = active
        fac[:, part] = up * sig * (1.0 + gate * (1.0 - sig))
        hid[:, part] = (active * up).astype(BF16)

    loads[2].wait()
    pack(lambda b: nt(hid[...], wd[Q * b : Q * b + Q, :]), send.at[2])
    whole(1).wait_send()
    copies(2, True, send.at[2], recv.at[2])

    whole(1).wait_recv()
    unpack(recv.at[1], cs)

    @pl.loop(0, FF // 256)
    def _(n):
        part = pl.ds(pl.multiple_of(n * 256, 256), 256)
        grad_hidden = nn(cs[...], wd[:, part])
        gu[:, part] = (grad_hidden * act[:, part]).astype(BF16)
        gg[:, part] = (grad_hidden * fac[:, part]).astype(BF16)

    def weight_terms(owner):
        part = pl.ds(pl.multiple_of(owner * CS, CS), CS)
        return (
            tn(xs[:, part], gg[...]),
            tn(xs[:, part], gu[...]),
            tn(cs[:, part], hid[...]),
        )

    over = []
    for j, dy in enumerate(DYS):
        terms = weight_terms(((y + dy) % NY) * 2 + 1 - core)
        for i in range(3):
            po[j, :, FF * i : FF * i + FF] = terms[i].astype(BF16)
        copy = pltpu.make_async_remote_copy(
            src_ref=po.at[j],
            dst_ref=pr.at[j],
            send_sem=po_sem.at[j],
            recv_sem=pr_sem.at[j],
            device_id=(sibling, me),
            device_id_type=MESH,
        )
        copy.start()
        over.append(copy)

    pack(
        lambda b: nt(gg[...], wg[Q * b : Q * b + Q, :]) + nt(gu[...], wu[Q * b : Q * b + Q, :]),
        send.at[3],
    )
    copies(3, True, send.at[3], recv.at[3])

    def along(i, src, dst, to):
        return pltpu.make_async_remote_copy(
            src_ref=src,
            dst_ref=dst,
            send_sem=y_send.at[i],
            recv_sem=y_recv.at[i],
            device_id=(to, me),
            device_id_type=MESH,
        )

    top, low = pl.ds(0, HALF), pl.ds(HALF, HALF)
    hops = [
        along(0, st.at[0, top], ra, y_next),
        along(1, st.at[0, low], rb, y_prev),
        along(2, st.at[1, low], r1.at[low], y_next),
        along(3, st.at[2, top], r3.at[top], y_prev),
        along(4, st.at[1, top], r1.at[top], y_next),
        along(5, st.at[2, low], r3.at[low], y_prev),
    ]
    for j, dy in enumerate(DYS[:3]):
        terms = weight_terms(((y + dy) % NY) * 2 + core)
        over[j].wait_recv()
        for i in range(3):
            part = slice(FF * i, FF * i + FF)
            st[j, :, part] = (terms[i] + pr[j, :, part].astype(F32)).astype(BF16)
        if j == 0:
            hops[0].start()
            hops[1].start()
        else:
            hops[1 + j].start()
    hops[0].wait_recv()
    st[1, top, :] = (st[1, top, :].astype(F32) + ra[...].astype(F32)).astype(BF16)
    hops[4].start()
    hops[1].wait_recv()
    st[2, low, :] = (st[2, low, :].astype(F32) + rb[...].astype(F32)).astype(BF16)
    hops[5].start()

    lane_s = iota((T, ROWS), 1)
    s_pick = [bits(lane_s == s_col[k]) for k in range(2)]
    v_pick = [[bits(lane_s + ROWS * b == v_col[k]) for b in range(3)] for k in range(2)]
    whole(2).wait_recv()
    sums = [jnp.zeros((T, 1), F32) for _ in range(2)]
    for b in range(4):
        total = jnp.zeros((T, Q), F32)
        cot = cotangent[:, Q * b : Q * b + Q].astype(F32)
        for k in range(2):
            if b < 3:
                rows = nn(s_pick[k], recv[2, :, Q * b : Q * b + Q])
            else:
                rows = nn(v_pick[k][0], recv[2, :, 0:Q])
                rows = rows + nn(v_pick[k][1], recv[2, :, Q : 2 * Q])
                rows = rows + nn(v_pick[k][2], recv[2, :, 2 * Q : W])
            total = total + combine[:, k : k + 1] * rows
            sums[k] = sums[k] + jnp.sum(cot * rows, axis=1, keepdims=True)
        mixed_out[:, Q * b : Q * b + Q] = total.astype(BF16)
    cgrad_out[...] = jnp.where(iota((T, 2), 1) == 0, sums[0], sums[1])

    terms = weight_terms(c)
    over[3].wait_recv()
    for i in (2, 3, 4, 5):
        hops[i].wait_recv()
    for i, out in enumerate((gate_out, up_out, down_out)):
        part = slice(FF * i, FF * i + FF)
        total = terms[i] + pr[3, :, part].astype(F32) + r1[:, part].astype(F32) + r3[:, part].astype(F32)
        out[0] = (total * grad_scale).astype(BF16)

    s_both = bits((lane_s == s_col[0]) | (lane_s == s_col[1]))
    whole(3).wait_recv()
    for b in range(3):
        igrad_out[:, Q * b : Q * b + Q] = nn(s_both, recv[3, :, Q * b : Q * b + Q]).astype(BF16)
    tail = jnp.zeros((T, Q), F32)
    for b in range(3):
        v_both = bits((lane_s + ROWS * b == v_col[0]) | (lane_s + ROWS * b == v_col[1]))
        tail = tail + nn(v_both, recv[3, :, Q * b : Q * b + Q])
    igrad_out[:, W:] = tail.astype(BF16)

    whole(2).wait_send()
    whole(3).wait_send()
    for copy in over:
        copy.wait_send()
    for copy in hops:
        copy.wait_send()


def local(hits, cotangent, combine, expert_ids, gate_weight, up_weight, down_weight):
    vmem = pl.BlockSpec(memory_space=pltpu.VMEM)
    hbm = pl.BlockSpec(memory_space=pl.ANY)
    shape = jax.ShapeDtypeStruct
    return pl.pallas_call(
        kernel,
        out_shape=(
            shape((T, D), BF16),
            shape((T, D), BF16),
            shape((T, 2), F32),
            shape((1, CS, FF), BF16),
            shape((1, CS, FF), BF16),
            shape((1, CS, FF), BF16),
        ),
        in_specs=[vmem, vmem, vmem, vmem, hbm, hbm, hbm],
        out_specs=(vmem,) * 6,
        scratch_shapes=[
            pltpu.VMEM((D, FF), BF16),
            pltpu.VMEM((D, FF), BF16),
            pltpu.VMEM((D, FF), BF16),
            pltpu.VMEM((4, ROWS, W), BF16),
            pltpu.VMEM((4, ROWS, W), BF16),
            pltpu.VMEM((ROWS, D), BF16),
            pltpu.VMEM((ROWS, D), BF16),
            pltpu.VMEM((ROWS, FF), F32),
            pltpu.VMEM((ROWS, FF), F32),
            pltpu.VMEM((ROWS, FF), BF16),
            pltpu.VMEM((ROWS, FF), BF16),
            pltpu.VMEM((ROWS, FF), BF16),
            pltpu.VMEM((4, CS, 3 * FF), BF16),
            pltpu.VMEM((4, CS, 3 * FF), BF16),
            pltpu.VMEM((3, CS, 3 * FF), BF16),
            pltpu.VMEM((HALF, 3 * FF), BF16),
            pltpu.VMEM((HALF, 3 * FF), BF16),
            pltpu.VMEM((CS, 3 * FF), BF16),
            pltpu.VMEM((CS, 3 * FF), BF16),
            pltpu.SemaphoreType.DMA((3,)),
            pltpu.SemaphoreType.DMA((4,)),
            pltpu.SemaphoreType.DMA((4,)),
            pltpu.SemaphoreType.DMA((4,)),
            pltpu.SemaphoreType.DMA((4,)),
            pltpu.SemaphoreType.DMA((6,)),
            pltpu.SemaphoreType.DMA((6,)),
        ],
        compiler_params=pltpu.CompilerParams(
            collective_id=0, has_side_effects=True, vmem_limit_bytes=64 << 20
        ),
        name="expert_step",
    )(hits, cotangent, combine, expert_ids, gate_weight, up_weight, down_weight)


def solution(mesh):
    rows = P(("ctx", "exp"), None)
    placed = (rows, rows, rows, rows, P("exp", None, None), P("exp", None, None), P("exp", None, None))
    outs = (rows, rows, rows, P("exp", "ctx", None), P("exp", "ctx", None), P("exp", "ctx", None))
    return jax.shard_map(local, mesh=mesh, in_specs=placed, out_specs=outs, check_vma=False)
```

```python
import functools

import jax
import jax.numpy as jnp
from jax import lax
from jax.experimental import pallas as pl
from jax.experimental.pallas import tpu as pltpu
from jax.sharding import PartitionSpec as P

MESH = pl.DeviceIdType.MESH
F32 = jnp.float32
BF16 = jnp.bfloat16

grad_scale = 0.0625
NZ, NX, NY = 8, 4, 4
EXPERTS = NZ * NX
CAP = 12
T = 128
D = 2048
FF = 768
RB = 16
Q = 512
W = 3 * Q
ROWS = EXPERTS * RB
CS = D // 8
HALF = CS // 2
DYS = (2, 1, 3, 0)


def shift_order():
    order = []
    for dx in range(NX):
        for dz in (1, 7, 2, 6, 3, 5, 4, 0):
            if (dz, dx) != (0, 0):
                order.append((dz, dx))
    return order


def nn(a, b):
    return jnp.dot(a, b, preferred_element_type=F32)


def nt(a, b):
    return lax.dot_general(a, b, (((1,), (1,)), ((), ())), preferred_element_type=F32)


def tn(a, b):
    return lax.dot_general(a, b, (((0,), (0,)), ((), ())), preferred_element_type=F32)


def iota(shape, dim):
    return lax.broadcasted_iota(jnp.int32, shape, dim)


def bits(cond):
    return jnp.where(cond, 1.0, 0.0).astype(BF16)


def kernel(
    hits, cotangent, combine, expert_ids, wg_hbm, wu_hbm, wd_hbm,
    mixed_out, igrad_out, cgrad_out, gate_out, up_out, down_out,
    wg, wu, wd, send, recv, xs, cs, act, fac, hid, gg, gu,
    po, pr, st, ra, rb, r1, r3,
    mixed, igrad, cgrad, gate, up, down,
    w_sem, send_sem, recv_sem, po_sem, pr_sem, y_send, y_recv, out_sem,
):
    c = lax.axis_index("ctx")
    me = lax.axis_index("exp")
    z, x = me // NX, me % NX
    y, core = c // 2, c % 2
    sibling = y * 2 + 1 - core
    y_next = ((y + 1) % NY) * 2 + core
    y_prev = ((y + NY - 1) % NY) * 2 + core
    order = shift_order()

    def peer(dz, dx):
        return ((z + dz) % NZ) * NX + (x + dx) % NX

    loads = []
    for i, (src, dst) in enumerate(((wg_hbm, wg), (wu_hbm, wu), (wd_hbm, wd))):
        copy = pltpu.make_async_copy(src.at[0], dst, w_sem.at[i])
        copy.start()
        loads.append(copy)

    barrier = pltpu.get_barrier_semaphore()
    for dz, dx in order:
        pl.semaphore_signal(barrier, inc=1, device_id=(c, peer(dz, dx)), device_id_type=MESH)
    for other in (sibling, y_next, y_prev):
        pl.semaphore_signal(barrier, inc=1, device_id=(other, me), device_id_type=MESH)

    name = iota((EXPERTS, T), 0)
    ids = [expert_ids[k : k + 1, :] for k in range(2)]
    named = bits((name == ids[0]) | (name == ids[1]))
    earlier = bits(iota((T, T), 0) < iota((T, T), 1))
    before = nn(named, earlier)
    s_row, v_row = [], []
    for k in range(2):
        rank = jnp.sum(jnp.where(name == ids[k], before, 0.0), axis=0, keepdims=True).astype(jnp.int32)
        block = (((ids[k] >> 2) - z) & (NZ - 1)) * NX + (((ids[k] & (NX - 1)) - x) & (NX - 1))
        s_row.append(block * RB + rank)
        v_row.append((rank >> 2) * ROWS + block * RB + CAP + (rank & 3))
    meta = jnp.concatenate(
        [r.astype(F32) for r in s_row + v_row] + [combine[0:1, :], combine[1:2, :], jnp.zeros((2, T), F32)],
        axis=0,
    )
    turned = jnp.transpose(jnp.concatenate([meta] * (T // 8), axis=0))
    s_col = [turned[:, k : k + 1].astype(jnp.int32) for k in range(2)]
    v_col = [turned[:, 2 + k : 3 + k].astype(jnp.int32) for k in range(2)]
    weights = [turned[:, 4 + k : 5 + k] for k in range(2)]
    rows_t = iota((ROWS, T), 0)

    def copies(phase, back, src, dst):
        for dz, dx in order:
            i = dz * NX + dx
            to = peer(NZ - dz, NX - dx) if back else peer(dz, dx)
            pltpu.make_async_remote_copy(
                src_ref=src.at[pl.ds(RB * i, RB)],
                dst_ref=dst.at[pl.ds(RB * i, RB)],
                send_sem=send_sem.at[phase],
                recv_sem=recv_sem.at[phase],
                device_id=(c, to),
                device_id_type=MESH,
            ).start()
        dst[0:RB, :] = src[0:RB, :]

    def whole(phase):
        return pltpu.make_async_remote_copy(
            src_ref=send.at[phase, pl.ds(RB, ROWS - RB)],
            dst_ref=recv.at[phase, pl.ds(RB, ROWS - RB)],
            send_sem=send_sem.at[phase],
            recv_sem=recv_sem.at[phase],
            device_id=(c, peer(1, 0)),
            device_id_type=MESH,
        )

    left_over = []

    def leave(i, src, dst):
        copy = pltpu.make_async_copy(src, dst, out_sem.at[i])
        copy.start()
        left_over.append(copy)

    d_any = bits((rows_t == s_row[0]) | (rows_t == s_row[1]))
    for b in range(3):
        t_any = bits((rows_t + ROWS * b == v_row[0]) | (rows_t + ROWS * b == v_row[1]))
        left = jnp.concatenate([d_any, t_any], axis=1)
        right = jnp.concatenate([hits[:, Q * b : Q * b + Q], hits[:, W:]], axis=0)
        send[0, :, Q * b : Q * b + Q] = nn(left, right).astype(BF16)
    pl.semaphore_wait(barrier, len(order) + 3)
    copies(0, False, send.at[0], recv.at[0])

    for b in range(3):
        left, right = [], []
        for k in range(2):
            weight = weights[k]
            left.append(bits(rows_t == s_row[k]))
            right.append((weight * cotangent[:, Q * b : Q * b + Q].astype(F32)).astype(BF16))
            left.append(bits(rows_t + ROWS * b == v_row[k]))
            right.append((weight * cotangent[:, W:].astype(F32)).astype(BF16))
        send[1, :, Q * b : Q * b + Q] = nn(
            jnp.concatenate(left, axis=1), jnp.concatenate(right, axis=0)
        ).astype(BF16)
    whole(0).wait_send()
    copies(1, False, send.at[1], recv.at[1])

    row = iota((256, 256), 0)
    col = iota((256, 256), 1)
    same = (row >> 4) == (col >> 4)
    keep = jnp.where((iota((256, 1), 0) & 15) < CAP, 1.0, 0.0)
    keep_all = jnp.where((iota((ROWS, 1), 0) & 15) < CAP, 1.0, 0.0)

    def unpack(src, dst):
        for h in range(ROWS // 256):
            part = pl.ds(256 * h, 256)
            tail = jnp.zeros((256, Q), F32)
            for b in range(3):
                block = src[part, Q * b : Q * b + Q]
                dst[part, Q * b : Q * b + Q] = (block.astype(F32) * keep).astype(BF16)
                pick = bits(
                    same & ((row & 15) < CAP) & (((row & 15) >> 2) == b) & ((col & 15) == CAP + (row & 3))
                )
                tail = tail + nn(pick, block)
            dst[part, W:] = tail.astype(BF16)

    def pack(product, dst):
        tail = product(3).astype(BF16)
        for b in range(3):
            main = product(b) * keep_all
            pick = bits(same & ((row & 15) >= CAP) & ((col & 15) == 4 * b + (row & 15) - CAP))
            for h in range(ROWS // 256):
                dst[256 * h : 256 * h + 256, Q * b : Q * b + Q] = (
                    main[256 * h : 256 * h + 256] + nn(pick, tail[256 * h : 256 * h + 256])
                ).astype(BF16)

    whole(0).wait_recv()
    unpack(recv.at[0], xs)
    loads[0].wait()
    loads[1].wait()

    @pl.loop(0, FF // 256)
    def _(n):
        part = pl.ds(pl.multiple_of(n * 256, 256), 256)
        gates = nn(xs[...], wg[:, part])
        ups = nn(xs[...], wu[:, part])
        sig = jax.nn.sigmoid(gates)
        active = gates * sig
        act[:, part] = active
        fac[:, part] = ups * sig * (1.0 + gates * (1.0 - sig))
        hid[:, part] = (active * ups).astype(BF16)

    loads[2].wait()
    pack(lambda b: nt(hid[...], wd[Q * b : Q * b + Q, :]), send.at[2])
    whole(1).wait_send()
    copies(2, True, send.at[2], recv.at[2])

    whole(1).wait_recv()
    unpack(recv.at[1], cs)

    @pl.loop(0, FF // 256)
    def _(n):
        part = pl.ds(pl.multiple_of(n * 256, 256), 256)
        grad_hidden = nn(cs[...], wd[:, part])
        gu[:, part] = (grad_hidden * act[:, part]).astype(BF16)
        gg[:, part] = (grad_hidden * fac[:, part]).astype(BF16)

    def weight_terms(owner):
        part = pl.ds(pl.multiple_of(owner * CS, CS), CS)
        return (
            tn(xs[:, part], gg[...]),
            tn(xs[:, part], gu[...]),
            tn(cs[:, part], hid[...]),
        )

    over = []
    for j, dy in enumerate(DYS):
        terms = weight_terms(((y + dy) % NY) * 2 + 1 - core)
        for i in range(3):
            po[j, :, FF * i : FF * i + FF] = terms[i].astype(BF16)
        copy = pltpu.make_async_remote_copy(
            src_ref=po.at[j],
            dst_ref=pr.at[j],
            send_sem=po_sem.at[j],
            recv_sem=pr_sem.at[j],
            device_id=(sibling, me),
            device_id_type=MESH,
        )
        copy.start()
        over.append(copy)

    pack(
        lambda b: nt(gg[...], wg[Q * b : Q * b + Q, :]) + nt(gu[...], wu[Q * b : Q * b + Q, :]),
        send.at[3],
    )
    copies(3, True, send.at[3], recv.at[3])

    def along(i, src, dst, to):
        return pltpu.make_async_remote_copy(
            src_ref=src,
            dst_ref=dst,
            send_sem=y_send.at[i],
            recv_sem=y_recv.at[i],
            device_id=(to, me),
            device_id_type=MESH,
        )

    top, low = pl.ds(0, HALF), pl.ds(HALF, HALF)
    hops = [
        along(0, st.at[0, top], ra, y_next),
        along(1, st.at[0, low], rb, y_prev),
        along(2, st.at[1, low], r1.at[low], y_next),
        along(3, st.at[2, top], r3.at[top], y_prev),
        along(4, st.at[1, top], r1.at[top], y_next),
        along(5, st.at[2, low], r3.at[low], y_prev),
    ]
    for j, dy in enumerate(DYS[:3]):
        terms = weight_terms(((y + dy) % NY) * 2 + core)
        over[j].wait_recv()
        for i in range(3):
            part = slice(FF * i, FF * i + FF)
            st[j, :, part] = (terms[i] + pr[j, :, part].astype(F32)).astype(BF16)
        if j == 0:
            hops[0].start()
            hops[1].start()
        else:
            hops[1 + j].start()
    hops[0].wait_recv()
    st[1, top, :] = (st[1, top, :].astype(F32) + ra[...].astype(F32)).astype(BF16)
    hops[4].start()
    hops[1].wait_recv()
    st[2, low, :] = (st[2, low, :].astype(F32) + rb[...].astype(F32)).astype(BF16)
    hops[5].start()

    lane_s = iota((T, ROWS), 1)
    s_pick = [bits(lane_s == s_col[k]) for k in range(2)]
    v_pick = [[bits(lane_s + ROWS * b == v_col[k]) for b in range(3)] for k in range(2)]
    whole(2).wait_recv()
    sums = [jnp.zeros((T, 1), F32) for _ in range(2)]
    for b in range(4):
        total = jnp.zeros((T, Q), F32)
        cot = cotangent[:, Q * b : Q * b + Q].astype(F32)
        for k in range(2):
            if b < 3:
                rows = nn(s_pick[k], recv[2, :, Q * b : Q * b + Q])
            else:
                rows = nn(v_pick[k][0], recv[2, :, 0:Q])
                rows = rows + nn(v_pick[k][1], recv[2, :, Q : 2 * Q])
                rows = rows + nn(v_pick[k][2], recv[2, :, 2 * Q : W])
            total = total + weights[k] * rows
            sums[k] = sums[k] + jnp.sum(cot * rows, axis=1, keepdims=True)
        mixed[:, Q * b : Q * b + Q] = total.astype(BF16)
    leave(0, mixed, mixed_out)
    cgrad[...] = jnp.transpose(jnp.where(iota((T, 128), 1) == 0, sums[0], sums[1]))[0:2, :]
    leave(1, cgrad, cgrad_out)

    terms = weight_terms(c)
    over[3].wait_recv()
    for i in (2, 3, 4, 5):
        hops[i].wait_recv()
    for i, (out, dst) in enumerate(((gate, gate_out), (up, up_out), (down, down_out))):
        part = slice(FF * i, FF * i + FF)
        total = terms[i] + pr[3, :, part].astype(F32) + r1[:, part].astype(F32) + r3[:, part].astype(F32)
        out[0] = (total * grad_scale).astype(BF16)
        leave(2 + i, out, dst)

    s_both = bits((lane_s == s_col[0]) | (lane_s == s_col[1]))
    whole(3).wait_recv()
    for b in range(3):
        igrad[:, Q * b : Q * b + Q] = nn(s_both, recv[3, :, Q * b : Q * b + Q]).astype(BF16)
    tail = jnp.zeros((T, Q), F32)
    for b in range(3):
        v_both = bits((lane_s + ROWS * b == v_col[0]) | (lane_s + ROWS * b == v_col[1]))
        tail = tail + nn(v_both, recv[3, :, Q * b : Q * b + Q])
    igrad[:, W:] = tail.astype(BF16)
    leave(5, igrad, igrad_out)

    whole(2).wait_send()
    whole(3).wait_send()
    for copy in over:
        copy.wait_send()
    for copy in hops:
        copy.wait_send()
    for copy in left_over:
        copy.wait()


def results(*refs):
    ins, outs, held, sem = refs[:6], refs[6:12], refs[12:18], refs[18]
    inward = [pltpu.make_async_copy(ins[i], held[i], sem.at[0, i]) for i in range(6)]
    outward = [pltpu.make_async_copy(held[i], outs[i], sem.at[1, i]) for i in range(6)]
    for copy in inward:
        copy.start()
    for before, after in zip(inward, outward):
        before.wait()
        after.start()
    for copy in outward:
        copy.wait()


def local(hits, cotangent, combine, expert_ids, gate_weight, up_weight, down_weight):
    vmem = pl.BlockSpec(memory_space=pltpu.VMEM)
    hbm = pl.BlockSpec(memory_space=pl.ANY)
    shape = jax.ShapeDtypeStruct
    kinds = (
        ((T, D), BF16),
        ((T, D), BF16),
        ((2, T), F32),
        ((1, CS, FF), BF16),
        ((1, CS, FF), BF16),
        ((1, CS, FF), BF16),
    )
    outs = tuple(shape(*kind) for kind in kinds)
    parts = pl.pallas_call(
        kernel,
        out_shape=outs,
        in_specs=[vmem, vmem, vmem, vmem, hbm, hbm, hbm],
        out_specs=(hbm,) * 6,
        scratch_shapes=[
            pltpu.VMEM((D, FF), BF16),
            pltpu.VMEM((D, FF), BF16),
            pltpu.VMEM((D, FF), BF16),
            pltpu.VMEM((4, ROWS, W), BF16),
            pltpu.VMEM((4, ROWS, W), BF16),
            pltpu.VMEM((ROWS, D), BF16),
            pltpu.VMEM((ROWS, D), BF16),
            pltpu.VMEM((ROWS, FF), F32),
            pltpu.VMEM((ROWS, FF), F32),
            pltpu.VMEM((ROWS, FF), BF16),
            pltpu.VMEM((ROWS, FF), BF16),
            pltpu.VMEM((ROWS, FF), BF16),
            pltpu.VMEM((4, CS, 3 * FF), BF16),
            pltpu.VMEM((4, CS, 3 * FF), BF16),
            pltpu.VMEM((3, CS, 3 * FF), BF16),
            pltpu.VMEM((HALF, 3 * FF), BF16),
            pltpu.VMEM((HALF, 3 * FF), BF16),
            pltpu.VMEM((CS, 3 * FF), BF16),
            pltpu.VMEM((CS, 3 * FF), BF16),
            *[pltpu.VMEM(*kind) for kind in kinds],
            pltpu.SemaphoreType.DMA((3,)),
            pltpu.SemaphoreType.DMA((4,)),
            pltpu.SemaphoreType.DMA((4,)),
            pltpu.SemaphoreType.DMA((4,)),
            pltpu.SemaphoreType.DMA((4,)),
            pltpu.SemaphoreType.DMA((6,)),
            pltpu.SemaphoreType.DMA((6,)),
            pltpu.SemaphoreType.DMA((6,)),
        ],
        compiler_params=pltpu.CompilerParams(
            collective_id=0, has_side_effects=True, vmem_limit_bytes=64 << 20
        ),
        name="expert_step",
    )(hits, cotangent, combine.T, expert_ids.T, gate_weight, up_weight, down_weight)
    mixed, igrad, cgrad, gate, up, down = pl.pallas_call(
        results,
        out_shape=outs,
        in_specs=[hbm] * 6,
        out_specs=(hbm,) * 6,
        scratch_shapes=[*[pltpu.VMEM(*kind) for kind in kinds], pltpu.SemaphoreType.DMA((2, 6))],
        name="results",
    )(*parts)
    return mixed, igrad, cgrad.T, gate, up, down


def solution(mesh):
    rows = P(("ctx", "exp"), None)
    placed = (rows, rows, rows, rows, P("exp", None, None), P("exp", None, None), P("exp", None, None))
    outs = (rows, rows, rows, P("exp", "ctx", None), P("exp", "ctx", None), P("exp", "ctx", None))
    return jax.shard_map(local, mesh=mesh, in_specs=placed, out_specs=outs, check_vma=False)
```

```python
import functools

import jax
import jax.numpy as jnp
from jax import lax
from jax.experimental import pallas as pl
from jax.experimental.pallas import tpu as pltpu
from jax.sharding import PartitionSpec as P

MESH = pl.DeviceIdType.MESH
F32 = jnp.float32
BF16 = jnp.bfloat16

grad_scale = 0.0625
NZ, NX, NY = 8, 4, 4
EXPERTS = NZ * NX
CAP = 12
T = 128
D = 2048
FF = 768
RB = 16
Q = 512
W = 3 * Q
ROWS = EXPERTS * RB
CS = D // 8
HALF = CS // 2
DYS = (2, 1, 3, 0)


GROUPS = ((0, 64), (64, 288), (288, 512))
WINDOWS = ((0, 128), (32, 256), (256, 256))
SAME = (0, 4, 28)


def hops_of():
    table = {}
    for dz in range(NZ):
        for dx in range(NX):
            i = dz * NX + dx
            if dz == 0:
                table[i] = (0, dx)
            elif i * RB < GROUPS[1][1]:
                table[i] = (dz - 1, dx)
            else:
                table[i] = (dz - NZ + 1, dx)
    order = []
    for dx in range(NX):
        for dz in (4, 3, 5, 2, 6, 1, 7, 0):
            order.append(dz * NX + dx)
    return [(i,) + table[i] for i in order if i not in SAME]


def nn(a, b):
    return jnp.dot(a, b, preferred_element_type=F32)


def nt(a, b):
    return lax.dot_general(a, b, (((1,), (1,)), ((), ())), preferred_element_type=F32)


def tn(a, b):
    return lax.dot_general(a, b, (((0,), (0,)), ((), ())), preferred_element_type=F32)


def iota(shape, dim):
    return lax.broadcasted_iota(jnp.int32, shape, dim)


def bits(cond):
    return jnp.where(cond, 1.0, 0.0).astype(BF16)


def kernel(
    hits, cotangent, combine, expert_ids, wg_hbm, wu_hbm, wd_hbm,
    mixed_out, igrad_out, cgrad_out, gate_out, up_out, down_out,
    wg, wu, wd, send, recv, xs, cs, act, fac, hid, gg, gu,
    po, pr, st, ra, rb, r1, r3,
    mixed, igrad, cgrad, gate, up, down,
    metas, raw, own, part_to, part_from, cg_to, cg_from,
    w_sem, send_sem, recv_sem, po_sem, pr_sem, y_send, y_recv, out_sem,
    raw_send, raw_recv, meta_send, meta_recv, part_send, part_recv, cg_send, cg_recv,
):
    c = lax.axis_index("ctx")
    me = lax.axis_index("exp")
    z, x = me // NX, me % NX
    y, core = c // 2, c % 2
    sibling = y * 2 + 1 - core
    y_next = ((y + 1) % NY) * 2 + core
    y_prev = ((y + NY - 1) % NY) * 2 + core
    order = hops_of()

    def peer(dz, dx):
        return ((z + dz + NZ) % NZ) * NX + (x + dx + NX) % NX

    def remote(src, dst, ssem, rsem, ctx, exp):
        return pltpu.make_async_remote_copy(
            src_ref=src, dst_ref=dst, send_sem=ssem, recv_sem=rsem, device_id=(ctx, exp), device_id_type=MESH
        )

    loads = []
    for i, (src, dst) in enumerate(((wg_hbm, wg), (wu_hbm, wu), (wd_hbm, wd))):
        copy = pltpu.make_async_copy(src.at[0], dst, w_sem.at[i])
        copy.start()
        loads.append(copy)

    barrier = pltpu.get_barrier_semaphore()
    near = [(dz, dx) for dz in range(-3, 4) for dx in range(NX) if (dz, dx) != (0, 0)]
    for dz, dx in near:
        pl.semaphore_signal(barrier, inc=1, device_id=(c, peer(dz, dx)), device_id_type=MESH)
    for other in (sibling, y_next, y_prev):
        pl.semaphore_signal(barrier, inc=1, device_id=(other, me), device_id_type=MESH)

    name = iota((EXPERTS, T), 0)
    ids = [expert_ids[k : k + 1, :] for k in range(2)]
    named = bits((name == ids[0]) | (name == ids[1]))
    earlier = bits(iota((T, T), 0) < iota((T, T), 1))
    before = nn(named, earlier)
    slots, tails = [], []
    for k in range(2):
        rank = jnp.sum(jnp.where(name == ids[k], before, 0.0), axis=0, keepdims=True).astype(jnp.int32)
        block = (((ids[k] >> 2) - z) & (NZ - 1)) * NX + (((ids[k] & (NX - 1)) - x) & (NX - 1))
        slots.append(block * RB + rank)
        tails.append((rank >> 2) * ROWS + block * RB + CAP + (rank & 3))
    metas[0] = jnp.concatenate(
        [r.astype(F32) for r in slots + tails] + [combine[0:1, :], combine[1:2, :], jnp.zeros((2, T), F32)],
        axis=0,
    )

    sides = ((peer(1, 0), peer(-1, 0)), (peer(-1, 0), peer(1, 0)))
    metas_sent = [
        remote(metas.at[0], metas.at[1 + i], meta_send.at[i], meta_recv.at[i], c, sides[i][0]) for i in range(2)
    ]
    raw_sent = [
        [remote(src, raw.at[p, i], raw_send.at[p, i], raw_recv.at[p, i], c, sides[i][0]) for i in range(2)]
        for p, src in enumerate((hits, cotangent))
    ]
    parts_sent = [
        [
            remote(part_to.at[p, i], part_from.at[p, i], part_send.at[p, i], part_recv.at[p, i], c, sides[i][1])
            for i in range(2)
        ]
        for p in range(2)
    ]
    cg_sent = [remote(cg_to.at[i], cg_from.at[i], cg_send.at[i], cg_recv.at[i], c, sides[i][1]) for i in range(2)]

    def rows_of(g):
        meta = metas[g]
        return (
            [meta[k : k + 1, :].astype(jnp.int32) for k in range(2)],
            [meta[2 + k : 3 + k, :].astype(jnp.int32) for k in range(2)],
        )

    def columns_of(g):
        turned = jnp.transpose(jnp.concatenate([metas[g]] * (T // 8), axis=0))
        return (
            [turned[:, k : k + 1].astype(jnp.int32) for k in range(2)],
            [turned[:, 2 + k : 3 + k].astype(jnp.int32) for k in range(2)],
            [turned[:, 4 + k : 5 + k] for k in range(2)],
        )

    def copies(phase, back, blocks):
        for i, dz, dx in order:
            if i in blocks:
                to = peer(-dz, -dx) if back else peer(dz, dx)
                part = pl.ds(RB * i, RB)
                remote(
                    send.at[phase, part], recv.at[phase, part], send_sem.at[phase], recv_sem.at[phase], c, to
                ).start()
        for i in SAME:
            if i in blocks:
                recv[phase, RB * i : RB * i + RB, :] = send[phase, RB * i : RB * i + RB, :]

    def whole(phase):
        part = pl.ds(0, RB * len(order))
        return remote(
            send.at[phase, part], recv.at[phase, part], send_sem.at[phase], recv_sem.at[phase], c, peer(1, 0)
        )

    near_blocks = range(0, GROUPS[0][1] // RB)
    far_blocks = range(GROUPS[1][0] // RB, EXPERTS)

    def pack_hits(g, src):
        lo, hi = GROUPS[g]
        s_row, v_row = rows_of(g)
        rows = iota((hi - lo, T), 0) + lo
        d_any = bits((rows == s_row[0]) | (rows == s_row[1]))
        for b in range(3):
            t_any = bits((rows + ROWS * b == v_row[0]) | (rows + ROWS * b == v_row[1]))
            left = jnp.concatenate([d_any, t_any], axis=1)
            right = jnp.concatenate([src[:, Q * b : Q * b + Q], src[:, W:]], axis=0)
            send[0, lo:hi, Q * b : Q * b + Q] = nn(left, right).astype(BF16)

    def pack_cots(g, src):
        lo, hi = GROUPS[g]
        s_row, v_row = rows_of(g)
        weights = columns_of(g)[2]
        rows = iota((hi - lo, T), 0) + lo
        for b in range(3):
            left, right = [], []
            for k in range(2):
                left.append(bits(rows == s_row[k]))
                right.append((weights[k] * src[:, Q * b : Q * b + Q].astype(F32)).astype(BF16))
                left.append(bits(rows + ROWS * b == v_row[k]))
                right.append((weights[k] * src[:, W:].astype(F32)).astype(BF16))
            send[1, lo:hi, Q * b : Q * b + Q] = nn(
                jnp.concatenate(left, axis=1), jnp.concatenate(right, axis=0)
            ).astype(BF16)

    left_over = []

    def leave(i, src, dst):
        copy = pltpu.make_async_copy(src, dst, out_sem.at[i])
        copy.start()
        left_over.append(copy)

    pl.semaphore_wait(barrier, len(near) + 3)
    for i in range(2):
        metas_sent[i].start()
        raw_sent[0][i].start()
    pack_hits(0, hits)
    copies(0, False, near_blocks)
    pack_cots(0, cotangent)

    for i in range(2):
        metas_sent[i].wait_recv()
        raw_sent[0][i].wait_recv()
        if i == 0:
            raw_sent[1][0].start()
            raw_sent[1][1].start()
        pack_hits(1 + i, raw.at[0, i])
    copies(0, False, far_blocks)

    for i in range(2):
        raw_sent[1][i].wait_recv()
        pack_cots(1 + i, raw.at[1, i])
    whole(0).wait_send()
    copies(1, False, range(EXPERTS))

    row = iota((256, 256), 0)
    col = iota((256, 256), 1)
    same = (row >> 4) == (col >> 4)
    keep = jnp.where((iota((256, 1), 0) & 15) < CAP, 1.0, 0.0)
    keep_all = jnp.where((iota((ROWS, 1), 0) & 15) < CAP, 1.0, 0.0)

    def unpack(src, dst):
        for h in range(ROWS // 256):
            part = pl.ds(256 * h, 256)
            tail = jnp.zeros((256, Q), F32)
            for b in range(3):
                block = src[part, Q * b : Q * b + Q]
                dst[part, Q * b : Q * b + Q] = (block.astype(F32) * keep).astype(BF16)
                pick = bits(
                    same & ((row & 15) < CAP) & (((row & 15) >> 2) == b) & ((col & 15) == CAP + (row & 3))
                )
                tail = tail + nn(pick, block)
            dst[part, W:] = tail.astype(BF16)

    def pack(product, dst):
        tail = product(3).astype(BF16)
        for b in range(3):
            main = product(b) * keep_all
            pick = bits(same & ((row & 15) >= CAP) & ((col & 15) == 4 * b + (row & 15) - CAP))
            for h in range(ROWS // 256):
                dst[256 * h : 256 * h + 256, Q * b : Q * b + Q] = (
                    main[256 * h : 256 * h + 256] + nn(pick, tail[256 * h : 256 * h + 256])
                ).astype(BF16)

    whole(0).wait_recv()
    unpack(recv.at[0], xs)
    loads[0].wait()
    loads[1].wait()

    @pl.loop(0, FF // 256)
    def _(n):
        part = pl.ds(pl.multiple_of(n * 256, 256), 256)
        gates = nn(xs[...], wg[:, part])
        ups = nn(xs[...], wu[:, part])
        sig = jax.nn.sigmoid(gates)
        active = gates * sig
        act[:, part] = active
        fac[:, part] = ups * sig * (1.0 + gates * (1.0 - sig))
        hid[:, part] = (active * ups).astype(BF16)

    loads[2].wait()
    pack(lambda b: nt(hid[...], wd[Q * b : Q * b + Q, :]), send.at[2])
    whole(1).wait_send()
    copies(2, True, range(EXPERTS))

    whole(1).wait_recv()
    unpack(recv.at[1], cs)

    @pl.loop(0, FF // 256)
    def _(n):
        part = pl.ds(pl.multiple_of(n * 256, 256), 256)
        grad_hidden = nn(cs[...], wd[:, part])
        gu[:, part] = (grad_hidden * act[:, part]).astype(BF16)
        gg[:, part] = (grad_hidden * fac[:, part]).astype(BF16)

    def weight_terms(owner):
        part = pl.ds(pl.multiple_of(owner * CS, CS), CS)
        return (
            tn(xs[:, part], gg[...]),
            tn(xs[:, part], gu[...]),
            tn(cs[:, part], hid[...]),
        )

    over = []
    for j, dy in enumerate(DYS):
        terms = weight_terms(((y + dy) % NY) * 2 + 1 - core)
        for i in range(3):
            po[j, :, FF * i : FF * i + FF] = terms[i].astype(BF16)
        copy = remote(po.at[j], pr.at[j], po_sem.at[j], pr_sem.at[j], sibling, me)
        copy.start()
        over.append(copy)

    pack(
        lambda b: nt(gg[...], wg[Q * b : Q * b + Q, :]) + nt(gu[...], wu[Q * b : Q * b + Q, :]),
        send.at[3],
    )

    def along(i, src, dst, to):
        return remote(src, dst, y_send.at[i], y_recv.at[i], to, me)

    top, low = pl.ds(0, HALF), pl.ds(HALF, HALF)
    hops = [
        along(0, st.at[0, top], ra, y_next),
        along(1, st.at[0, low], rb, y_prev),
        along(2, st.at[1, low], r1.at[low], y_next),
        along(3, st.at[2, top], r3.at[top], y_prev),
        along(4, st.at[1, top], r1.at[top], y_next),
        along(5, st.at[2, low], r3.at[low], y_prev),
    ]
    for j, dy in enumerate(DYS[:3]):
        terms = weight_terms(((y + dy) % NY) * 2 + core)
        over[j].wait_recv()
        for i in range(3):
            part = slice(FF * i, FF * i + FF)
            st[j, :, part] = (terms[i] + pr[j, :, part].astype(F32)).astype(BF16)
        if j == 0:
            hops[0].start()
            hops[1].start()
            whole(2).wait_send()
            copies(3, True, range(EXPERTS))
        else:
            hops[1 + j].start()

    def picks(g):
        lo, hi = GROUPS[g]
        start, length = WINDOWS[g]
        s_col, v_col, weights = columns_of(g)
        lanes = iota((T, length), 1) + start
        s_pick, v_pick = [], []
        for k in range(2):
            inside = (s_col[k] >= lo) & (s_col[k] < hi)
            s_in = jnp.where(inside, s_col[k], -1)
            v_in = jnp.where(inside, v_col[k], -1)
            s_pick.append(lanes == s_in)
            v_pick.append([lanes + ROWS * b == v_in for b in range(3)])
        return s_pick, v_pick, weights

    whole(2).wait_recv()
    for g in (1, 2, 0):
        s_pick, v_pick, weights = picks(g)
        window = pl.ds(*WINDOWS[g])
        source = cotangent if g == 0 else raw.at[1, g - 1]
        sums = [jnp.zeros((T, 1), F32) for _ in range(2)]
        for b in range(4):
            total = jnp.zeros((T, Q), F32)
            cot = source[:, Q * b : Q * b + Q].astype(F32)
            for k in range(2):
                if b < 3:
                    rows = nn(bits(s_pick[k]), recv[2, window, Q * b : Q * b + Q])
                else:
                    rows = nn(bits(v_pick[k][0]), recv[2, window, 0:Q])
                    rows = rows + nn(bits(v_pick[k][1]), recv[2, window, Q : 2 * Q])
                    rows = rows + nn(bits(v_pick[k][2]), recv[2, window, 2 * Q : W])
                total = total + weights[k] * rows
                sums[k] = sums[k] + jnp.sum(cot * rows, axis=1, keepdims=True)
            if g == 0:
                own[0, :, Q * b : Q * b + Q] = total
            else:
                part_to[0, g - 1, :, Q * b : Q * b + Q] = total.astype(BF16)
        pair = jnp.transpose(jnp.where(iota((T, 128), 1) == 0, sums[0], sums[1]))[0:8, :]
        if g == 0:
            own_pair = pair
        else:
            cg_to[g - 1] = pair
            parts_sent[0][g - 1].start()
            cg_sent[g - 1].start()

    hops[0].wait_recv()
    st[1, top, :] = (st[1, top, :].astype(F32) + ra[...].astype(F32)).astype(BF16)
    hops[4].start()
    hops[1].wait_recv()
    st[2, low, :] = (st[2, low, :].astype(F32) + rb[...].astype(F32)).astype(BF16)
    hops[5].start()

    whole(3).wait_recv()
    for g in (1, 2, 0):
        s_pick, v_pick, _ = picks(g)
        window = pl.ds(*WINDOWS[g])
        s_both = bits(s_pick[0] | s_pick[1])
        v_both = [bits(v_pick[0][b] | v_pick[1][b]) for b in range(3)]
        for b in range(4):
            if b < 3:
                total = nn(s_both, recv[3, window, Q * b : Q * b + Q])
            else:
                total = nn(v_both[0], recv[3, window, 0:Q])
                total = total + nn(v_both[1], recv[3, window, Q : 2 * Q])
                total = total + nn(v_both[2], recv[3, window, 2 * Q : W])
            if g == 0:
                own[1, :, Q * b : Q * b + Q] = total
            else:
                part_to[1, g - 1, :, Q * b : Q * b + Q] = total.astype(BF16)
        if g > 0:
            parts_sent[1][g - 1].start()

    for i in range(2):
        parts_sent[0][i].wait_recv()
        cg_sent[i].wait_recv()
    mixed[...] = (own[0] + part_from[0, 0].astype(F32) + part_from[0, 1].astype(F32)).astype(BF16)
    leave(0, mixed, mixed_out)
    cgrad[...] = (own_pair + cg_from[0] + cg_from[1])[0:2, :]
    leave(1, cgrad, cgrad_out)

    terms = weight_terms(c)
    over[3].wait_recv()
    for i in (2, 3, 4, 5):
        hops[i].wait_recv()
    for i, (out, dst) in enumerate(((gate, gate_out), (up, up_out), (down, down_out))):
        part = slice(FF * i, FF * i + FF)
        total = terms[i] + pr[3, :, part].astype(F32) + r1[:, part].astype(F32) + r3[:, part].astype(F32)
        out[0] = (total * grad_scale).astype(BF16)
        leave(2 + i, out, dst)

    for i in range(2):
        parts_sent[1][i].wait_recv()
    igrad[...] = (own[1] + part_from[1, 0].astype(F32) + part_from[1, 1].astype(F32)).astype(BF16)
    leave(5, igrad, igrad_out)

    whole(3).wait_send()
    for copy in over + hops + metas_sent + cg_sent + sum(raw_sent + parts_sent, []):
        copy.wait_send()
    for copy in left_over:
        copy.wait()


def results(*refs):
    ins, outs, held, sem = refs[:6], refs[6:12], refs[12:18], refs[18]
    inward = [pltpu.make_async_copy(ins[i], held[i], sem.at[0, i]) for i in range(6)]
    outward = [pltpu.make_async_copy(held[i], outs[i], sem.at[1, i]) for i in range(6)]
    for copy in inward:
        copy.start()
    for before, after in zip(inward, outward):
        before.wait()
        after.start()
    for copy in outward:
        copy.wait()


def local(hits, cotangent, combine, expert_ids, gate_weight, up_weight, down_weight):
    vmem = pl.BlockSpec(memory_space=pltpu.VMEM)
    hbm = pl.BlockSpec(memory_space=pl.ANY)
    shape = jax.ShapeDtypeStruct
    kinds = (
        ((T, D), BF16),
        ((T, D), BF16),
        ((2, T), F32),
        ((1, CS, FF), BF16),
        ((1, CS, FF), BF16),
        ((1, CS, FF), BF16),
    )
    outs = tuple(shape(*kind) for kind in kinds)
    parts = pl.pallas_call(
        kernel,
        out_shape=outs,
        in_specs=[vmem, vmem, vmem, vmem, hbm, hbm, hbm],
        out_specs=(hbm,) * 6,
        scratch_shapes=[
            pltpu.VMEM((D, FF), BF16),
            pltpu.VMEM((D, FF), BF16),
            pltpu.VMEM((D, FF), BF16),
            pltpu.VMEM((4, ROWS, W), BF16),
            pltpu.VMEM((4, ROWS, W), BF16),
            pltpu.VMEM((ROWS, D), BF16),
            pltpu.VMEM((ROWS, D), BF16),
            pltpu.VMEM((ROWS, FF), F32),
            pltpu.VMEM((ROWS, FF), F32),
            pltpu.VMEM((ROWS, FF), BF16),
            pltpu.VMEM((ROWS, FF), BF16),
            pltpu.VMEM((ROWS, FF), BF16),
            pltpu.VMEM((4, CS, 3 * FF), BF16),
            pltpu.VMEM((4, CS, 3 * FF), BF16),
            pltpu.VMEM((3, CS, 3 * FF), BF16),
            pltpu.VMEM((HALF, 3 * FF), BF16),
            pltpu.VMEM((HALF, 3 * FF), BF16),
            pltpu.VMEM((CS, 3 * FF), BF16),
            pltpu.VMEM((CS, 3 * FF), BF16),
            *[pltpu.VMEM(*kind) for kind in kinds],
            pltpu.VMEM((3, 8, T), F32),
            pltpu.VMEM((2, 2, T, D), BF16),
            pltpu.VMEM((2, T, D), F32),
            pltpu.VMEM((2, 2, T, D), BF16),
            pltpu.VMEM((2, 2, T, D), BF16),
            pltpu.VMEM((2, 8, T), F32),
            pltpu.VMEM((2, 8, T), F32),
            pltpu.SemaphoreType.DMA((3,)),
            pltpu.SemaphoreType.DMA((4,)),
            pltpu.SemaphoreType.DMA((4,)),
            pltpu.SemaphoreType.DMA((4,)),
            pltpu.SemaphoreType.DMA((4,)),
            pltpu.SemaphoreType.DMA((6,)),
            pltpu.SemaphoreType.DMA((6,)),
            pltpu.SemaphoreType.DMA((6,)),
            pltpu.SemaphoreType.DMA((2, 2)),
            pltpu.SemaphoreType.DMA((2, 2)),
            pltpu.SemaphoreType.DMA((2,)),
            pltpu.SemaphoreType.DMA((2,)),
            pltpu.SemaphoreType.DMA((2, 2)),
            pltpu.SemaphoreType.DMA((2, 2)),
            pltpu.SemaphoreType.DMA((2,)),
            pltpu.SemaphoreType.DMA((2,)),
        ],
        compiler_params=pltpu.CompilerParams(
            collective_id=0, has_side_effects=True, vmem_limit_bytes=64 << 20
        ),
        name="expert_step",
    )(hits, cotangent, combine.T, expert_ids.T, gate_weight, up_weight, down_weight)
    mixed, igrad, cgrad, gate, up, down = pl.pallas_call(
        results,
        out_shape=outs,
        in_specs=[hbm] * 6,
        out_specs=(hbm,) * 6,
        scratch_shapes=[*[pltpu.VMEM(*kind) for kind in kinds], pltpu.SemaphoreType.DMA((2, 6))],
        name="results",
    )(*parts)
    return mixed, igrad, cgrad.T, gate, up, down


def solution(mesh):
    rows = P(("ctx", "exp"), None)
    placed = (rows, rows, rows, rows, P("exp", None, None), P("exp", None, None), P("exp", None, None))
    outs = (rows, rows, rows, P("exp", "ctx", None), P("exp", "ctx", None), P("exp", "ctx", None))
    return jax.shard_map(local, mesh=mesh, in_specs=placed, out_specs=outs, check_vma=False)
```

```python
import functools

import jax
import jax.numpy as jnp
from jax import lax
from jax.experimental import pallas as pl
from jax.experimental.pallas import tpu as pltpu
from jax.sharding import PartitionSpec as P

MESH = pl.DeviceIdType.MESH
F32 = jnp.float32
BF16 = jnp.bfloat16

grad_scale = 0.0625
NZ, NX, NY = 8, 4, 4
EXPERTS = NZ * NX
CAP = 12
T = 128
D = 2048
FF = 768
RB = 16
Q = 512
W = 3 * Q
ROWS = EXPERTS * RB
CS = D // 8
HALF = CS // 2
DYS = (2, 1, 3, 0)


GROUPS = ((0, 64), (64, 288), (288, 512))
WINDOWS = ((0, 128), (32, 256), (256, 256))
SAME = (0, 4, 28)


def hops_of():
    table = {}
    for dz in range(NZ):
        for dx in range(NX):
            i = dz * NX + dx
            if dz == 0:
                table[i] = (0, dx)
            elif i * RB < GROUPS[1][1]:
                table[i] = (dz - 1, dx)
            else:
                table[i] = (dz - NZ + 1, dx)
    order = []
    for dx in range(NX):
        for dz in (4, 3, 5, 2, 6, 1, 7, 0):
            order.append(dz * NX + dx)
    return [(i,) + table[i] for i in order if i not in SAME]


def nn(a, b):
    return jnp.dot(a, b, preferred_element_type=F32)


def nt(a, b):
    return lax.dot_general(a, b, (((1,), (1,)), ((), ())), preferred_element_type=F32)


def tn(a, b):
    return lax.dot_general(a, b, (((0,), (0,)), ((), ())), preferred_element_type=F32)


def iota(shape, dim):
    return lax.broadcasted_iota(jnp.int32, shape, dim)


def bits(cond):
    return jnp.where(cond, 1.0, 0.0).astype(BF16)


def kernel(
    hits, cotangent, combine, expert_ids, wg_hbm, wu_hbm, wd_hbm,
    mixed_out, igrad_out, cgrad_out, gate_out, up_out, down_out,
    wg, wu, wd, send, recv, xs, cs, act, fac, hid, gg, gu,
    po, pr, st, ra, rb, r1, r3,
    mixed, igrad, cgrad, gate, up, down,
    metas, raw, own, part_to, part_from, cg_to, cg_from,
    w_sem, send_sem, recv_sem, po_sem, pr_sem, y_send, y_recv, out_sem,
    raw_send, raw_recv, meta_send, meta_recv, part_send, part_recv, cg_send, cg_recv,
):
    c = lax.axis_index("ctx")
    me = lax.axis_index("exp")
    z, x = me // NX, me % NX
    y, core = c // 2, c % 2
    sibling = y * 2 + 1 - core
    y_next = ((y + 1) % NY) * 2 + core
    y_prev = ((y + NY - 1) % NY) * 2 + core
    order = hops_of()

    def peer(dz, dx):
        return ((z + dz + NZ) % NZ) * NX + (x + dx + NX) % NX

    def remote(src, dst, ssem, rsem, ctx, exp):
        return pltpu.make_async_remote_copy(
            src_ref=src, dst_ref=dst, send_sem=ssem, recv_sem=rsem, device_id=(ctx, exp), device_id_type=MESH
        )

    loads = []
    for i, (src, dst) in enumerate(((wg_hbm, wg), (wu_hbm, wu), (wd_hbm, wd))):
        copy = pltpu.make_async_copy(src.at[0], dst, w_sem.at[i])
        copy.start()
        loads.append(copy)

    barrier = pltpu.get_barrier_semaphore()
    near = [(dz, dx) for dz in range(-3, 4) for dx in range(NX) if (dz, dx) != (0, 0)]
    for dz, dx in near:
        pl.semaphore_signal(barrier, inc=1, device_id=(c, peer(dz, dx)), device_id_type=MESH)
    for other in (sibling, y_next, y_prev):
        pl.semaphore_signal(barrier, inc=1, device_id=(other, me), device_id_type=MESH)

    sides = ((peer(1, 0), peer(-1, 0)), (peer(-1, 0), peer(1, 0)))
    metas_sent = [
        remote(metas.at[0], metas.at[1 + i], meta_send.at[i], meta_recv.at[i], c, sides[i][0]) for i in range(2)
    ]
    raw_sent = [
        [remote(src, raw.at[p, i], raw_send.at[p, i], raw_recv.at[p, i], c, sides[i][0]) for i in range(2)]
        for p, src in enumerate((hits, cotangent))
    ]
    parts_sent = [
        [
            remote(part_to.at[p, i], part_from.at[p, i], part_send.at[p, i], part_recv.at[p, i], c, sides[i][1])
            for i in range(2)
        ]
        for p in range(2)
    ]
    cg_sent = [remote(cg_to.at[i], cg_from.at[i], cg_send.at[i], cg_recv.at[i], c, sides[i][1]) for i in range(2)]

    pl.semaphore_wait(barrier, len(near) + 3)
    for i in range(2):
        raw_sent[0][i].start()

    name = iota((EXPERTS, T), 0)
    ids = [expert_ids[k : k + 1, :] for k in range(2)]
    named = bits((name == ids[0]) | (name == ids[1]))
    earlier = bits(iota((T, T), 0) < iota((T, T), 1))
    before = nn(named, earlier)
    slots, tails = [], []
    for k in range(2):
        rank = jnp.sum(jnp.where(name == ids[k], before, 0.0), axis=0, keepdims=True).astype(jnp.int32)
        block = (((ids[k] >> 2) - z) & (NZ - 1)) * NX + (((ids[k] & (NX - 1)) - x) & (NX - 1))
        slots.append(block * RB + rank)
        tails.append((rank >> 2) * ROWS + block * RB + CAP + (rank & 3))
    metas[0] = jnp.concatenate(
        [r.astype(F32) for r in slots + tails] + [combine[0:1, :], combine[1:2, :], jnp.zeros((2, T), F32)],
        axis=0,
    )

    def rows_of(g):
        meta = metas[g]
        return (
            [meta[k : k + 1, :].astype(jnp.int32) for k in range(2)],
            [meta[2 + k : 3 + k, :].astype(jnp.int32) for k in range(2)],
        )

    def columns_of(g):
        turned = jnp.transpose(jnp.concatenate([metas[g]] * (T // 8), axis=0))
        return (
            [turned[:, k : k + 1].astype(jnp.int32) for k in range(2)],
            [turned[:, 2 + k : 3 + k].astype(jnp.int32) for k in range(2)],
            [turned[:, 4 + k : 5 + k] for k in range(2)],
        )

    def copies(phase, back, blocks):
        for i, dz, dx in order:
            if i in blocks:
                to = peer(-dz, -dx) if back else peer(dz, dx)
                part = pl.ds(RB * i, RB)
                remote(
                    send.at[phase, part], recv.at[phase, part], send_sem.at[phase], recv_sem.at[phase], c, to
                ).start()
        for i in SAME:
            if i in blocks:
                recv[phase, RB * i : RB * i + RB, :] = send[phase, RB * i : RB * i + RB, :]

    def whole(phase):
        part = pl.ds(0, RB * len(order))
        return remote(
            send.at[phase, part], recv.at[phase, part], send_sem.at[phase], recv_sem.at[phase], c, peer(1, 0)
        )

    near_blocks = range(0, GROUPS[0][1] // RB)
    far_blocks = range(GROUPS[1][0] // RB, EXPERTS)

    def pack_hits(g, src):
        lo, hi = GROUPS[g]
        s_row, v_row = rows_of(g)
        rows = iota((hi - lo, T), 0) + lo
        d_any = bits((rows == s_row[0]) | (rows == s_row[1]))
        for b in range(3):
            t_any = bits((rows + ROWS * b == v_row[0]) | (rows + ROWS * b == v_row[1]))
            left = jnp.concatenate([d_any, t_any], axis=1)
            right = jnp.concatenate([src[:, Q * b : Q * b + Q], src[:, W:]], axis=0)
            send[0, lo:hi, Q * b : Q * b + Q] = nn(left, right).astype(BF16)

    def pack_cots(g, src):
        lo, hi = GROUPS[g]
        s_row, v_row = rows_of(g)
        weights = columns_of(g)[2]
        rows = iota((hi - lo, T), 0) + lo
        for b in range(3):
            left, right = [], []
            for k in range(2):
                left.append(bits(rows == s_row[k]))
                right.append((weights[k] * src[:, Q * b : Q * b + Q].astype(F32)).astype(BF16))
                left.append(bits(rows + ROWS * b == v_row[k]))
                right.append((weights[k] * src[:, W:].astype(F32)).astype(BF16))
            send[1, lo:hi, Q * b : Q * b + Q] = nn(
                jnp.concatenate(left, axis=1), jnp.concatenate(right, axis=0)
            ).astype(BF16)

    left_over = []

    def leave(i, src, dst):
        copy = pltpu.make_async_copy(src, dst, out_sem.at[i])
        copy.start()
        left_over.append(copy)

    for i in range(2):
        metas_sent[i].start()
    pack_hits(0, hits)
    copies(0, False, near_blocks)
    pack_cots(0, cotangent)

    for i in range(2):
        metas_sent[i].wait_recv()
        raw_sent[0][i].wait_recv()
        if i == 0:
            raw_sent[1][0].start()
            raw_sent[1][1].start()
        pack_hits(1 + i, raw.at[0, i])
    copies(0, False, far_blocks)

    for i in range(2):
        raw_sent[1][i].wait_recv()
        pack_cots(1 + i, raw.at[1, i])
    whole(0).wait_send()
    copies(1, False, range(EXPERTS))

    row = iota((256, 256), 0)
    col = iota((256, 256), 1)
    same = (row >> 4) == (col >> 4)
    keep = jnp.where((iota((256, 1), 0) & 15) < CAP, 1.0, 0.0)
    keep_all = jnp.where((iota((ROWS, 1), 0) & 15) < CAP, 1.0, 0.0)

    def unpack(src, dst):
        for h in range(ROWS // 256):
            part = pl.ds(256 * h, 256)
            tail = jnp.zeros((256, Q), F32)
            for b in range(3):
                block = src[part, Q * b : Q * b + Q]
                dst[part, Q * b : Q * b + Q] = (block.astype(F32) * keep).astype(BF16)
                pick = bits(
                    same & ((row & 15) < CAP) & (((row & 15) >> 2) == b) & ((col & 15) == CAP + (row & 3))
                )
                tail = tail + nn(pick, block)
            dst[part, W:] = tail.astype(BF16)

    def pack(product, dst):
        tail = product(3).astype(BF16)
        for b in range(3):
            main = product(b) * keep_all
            pick = bits(same & ((row & 15) >= CAP) & ((col & 15) == 4 * b + (row & 15) - CAP))
            for h in range(ROWS // 256):
                dst[256 * h : 256 * h + 256, Q * b : Q * b + Q] = (
                    main[256 * h : 256 * h + 256] + nn(pick, tail[256 * h : 256 * h + 256])
                ).astype(BF16)

    whole(0).wait_recv()
    unpack(recv.at[0], xs)
    loads[0].wait()
    loads[1].wait()

    @pl.loop(0, FF // 256)
    def _(n):
        part = pl.ds(pl.multiple_of(n * 256, 256), 256)
        gates = nn(xs[...], wg[:, part])
        ups = nn(xs[...], wu[:, part])
        sig = jax.nn.sigmoid(gates)
        active = gates * sig
        act[:, part] = active
        fac[:, part] = ups * sig * (1.0 + gates * (1.0 - sig))
        hid[:, part] = (active * ups).astype(BF16)

    loads[2].wait()
    pack(lambda b: nt(hid[...], wd[Q * b : Q * b + Q, :]), send.at[2])
    copies(2, True, range(EXPERTS))
    whole(1).wait_send()

    whole(1).wait_recv()
    unpack(recv.at[1], cs)

    @pl.loop(0, FF // 256)
    def _(n):
        part = pl.ds(pl.multiple_of(n * 256, 256), 256)
        grad_hidden = nn(cs[...], wd[:, part])
        gu[:, part] = (grad_hidden * act[:, part]).astype(BF16)
        gg[:, part] = (grad_hidden * fac[:, part]).astype(BF16)

    def weight_terms(owner):
        part = pl.ds(pl.multiple_of(owner * CS, CS), CS)
        return (
            tn(xs[:, part], gg[...]),
            tn(xs[:, part], gu[...]),
            tn(cs[:, part], hid[...]),
        )

    pack(
        lambda b: nt(gg[...], wg[Q * b : Q * b + Q, :]) + nt(gu[...], wu[Q * b : Q * b + Q, :]),
        send.at[3],
    )

    copies(3, True, range(EXPERTS))

    over = []
    for j, dy in enumerate(DYS):
        terms = weight_terms(((y + dy) % NY) * 2 + 1 - core)
        for i in range(3):
            po[j, :, FF * i : FF * i + FF] = terms[i].astype(BF16)
        copy = remote(po.at[j], pr.at[j], po_sem.at[j], pr_sem.at[j], sibling, me)
        copy.start()
        over.append(copy)

    def along(i, src, dst, to):
        return remote(src, dst, y_send.at[i], y_recv.at[i], to, me)

    top, low = pl.ds(0, HALF), pl.ds(HALF, HALF)
    hops = [
        along(0, st.at[0, top], ra, y_next),
        along(1, st.at[0, low], rb, y_prev),
        along(2, st.at[1, low], r1.at[low], y_next),
        along(3, st.at[2, top], r3.at[top], y_prev),
        along(4, st.at[1, top], r1.at[top], y_next),
        along(5, st.at[2, low], r3.at[low], y_prev),
    ]
    for j, dy in enumerate(DYS[:3]):
        terms = weight_terms(((y + dy) % NY) * 2 + core)
        over[j].wait_recv()
        for i in range(3):
            part = slice(FF * i, FF * i + FF)
            st[j, :, part] = (terms[i] + pr[j, :, part].astype(F32)).astype(BF16)
        if j == 0:
            hops[0].start()
            hops[1].start()
        else:
            hops[1 + j].start()

    def picks(g):
        lo, hi = GROUPS[g]
        start, length = WINDOWS[g]
        s_col, v_col, weights = columns_of(g)
        lanes = iota((T, length), 1) + start
        s_pick, v_pick = [], []
        for k in range(2):
            inside = (s_col[k] >= lo) & (s_col[k] < hi)
            s_in = jnp.where(inside, s_col[k], -1)
            v_in = jnp.where(inside, v_col[k], -1)
            s_pick.append(lanes == s_in)
            v_pick.append([lanes + ROWS * b == v_in for b in range(3)])
        return s_pick, v_pick, weights

    whole(2).wait_recv()
    for g in (1, 2, 0):
        s_pick, v_pick, weights = picks(g)
        window = pl.ds(*WINDOWS[g])
        source = cotangent if g == 0 else raw.at[1, g - 1]
        sums = [jnp.zeros((T, 1), F32) for _ in range(2)]
        for b in range(4):
            total = jnp.zeros((T, Q), F32)
            cot = source[:, Q * b : Q * b + Q].astype(F32)
            for k in range(2):
                if b < 3:
                    rows = nn(bits(s_pick[k]), recv[2, window, Q * b : Q * b + Q])
                else:
                    rows = nn(bits(v_pick[k][0]), recv[2, window, 0:Q])
                    rows = rows + nn(bits(v_pick[k][1]), recv[2, window, Q : 2 * Q])
                    rows = rows + nn(bits(v_pick[k][2]), recv[2, window, 2 * Q : W])
                total = total + weights[k] * rows
                sums[k] = sums[k] + jnp.sum(cot * rows, axis=1, keepdims=True)
            if g == 0:
                own[0, :, Q * b : Q * b + Q] = total
            else:
                part_to[0, g - 1, :, Q * b : Q * b + Q] = total.astype(BF16)
        pair = jnp.transpose(jnp.where(iota((T, 128), 1) == 0, sums[0], sums[1]))[0:8, :]
        if g == 0:
            own_pair = pair
        else:
            cg_to[g - 1] = pair

    hops[0].wait_recv()
    st[1, top, :] = (st[1, top, :].astype(F32) + ra[...].astype(F32)).astype(BF16)
    hops[4].start()
    hops[1].wait_recv()
    st[2, low, :] = (st[2, low, :].astype(F32) + rb[...].astype(F32)).astype(BF16)
    hops[5].start()

    whole(2).wait_send()
    whole(3).wait_send()
    for i in range(2):
        parts_sent[0][i].start()
        cg_sent[i].start()

    whole(3).wait_recv()
    for g in (1, 2, 0):
        s_pick, v_pick, _ = picks(g)
        window = pl.ds(*WINDOWS[g])
        s_both = bits(s_pick[0] | s_pick[1])
        v_both = [bits(v_pick[0][b] | v_pick[1][b]) for b in range(3)]
        for b in range(4):
            if b < 3:
                total = nn(s_both, recv[3, window, Q * b : Q * b + Q])
            else:
                total = nn(v_both[0], recv[3, window, 0:Q])
                total = total + nn(v_both[1], recv[3, window, Q : 2 * Q])
                total = total + nn(v_both[2], recv[3, window, 2 * Q : W])
            if g == 0:
                own[1, :, Q * b : Q * b + Q] = total
            else:
                part_to[1, g - 1, :, Q * b : Q * b + Q] = total.astype(BF16)
        if g > 0:
            parts_sent[1][g - 1].start()

    for i in range(2):
        parts_sent[0][i].wait_recv()
        cg_sent[i].wait_recv()
    mixed[...] = (own[0] + part_from[0, 0].astype(F32) + part_from[0, 1].astype(F32)).astype(BF16)
    leave(0, mixed, mixed_out)
    cgrad[...] = (own_pair + cg_from[0] + cg_from[1])[0:2, :]
    leave(1, cgrad, cgrad_out)

    terms = weight_terms(c)
    over[3].wait_recv()
    for i in (2, 3, 4, 5):
        hops[i].wait_recv()
    for i, (out, dst) in enumerate(((gate, gate_out), (up, up_out), (down, down_out))):
        part = slice(FF * i, FF * i + FF)
        total = terms[i] + pr[3, :, part].astype(F32) + r1[:, part].astype(F32) + r3[:, part].astype(F32)
        out[0] = (total * grad_scale).astype(BF16)
        leave(2 + i, out, dst)

    for i in range(2):
        parts_sent[1][i].wait_recv()
    igrad[...] = (own[1] + part_from[1, 0].astype(F32) + part_from[1, 1].astype(F32)).astype(BF16)
    leave(5, igrad, igrad_out)

    for copy in over + hops + metas_sent + cg_sent + sum(raw_sent + parts_sent, []):
        copy.wait_send()
    for copy in left_over:
        copy.wait()


def results(*refs):
    ins, outs, held, sem = refs[:6], refs[6:12], refs[12:18], refs[18]
    inward = [pltpu.make_async_copy(ins[i], held[i], sem.at[0, i]) for i in range(6)]
    outward = [pltpu.make_async_copy(held[i], outs[i], sem.at[1, i]) for i in range(6)]
    for copy in inward:
        copy.start()
    for before, after in zip(inward, outward):
        before.wait()
        after.start()
    for copy in outward:
        copy.wait()


def local(hits, cotangent, combine, expert_ids, gate_weight, up_weight, down_weight):
    vmem = pl.BlockSpec(memory_space=pltpu.VMEM)
    hbm = pl.BlockSpec(memory_space=pl.ANY)
    shape = jax.ShapeDtypeStruct
    kinds = (
        ((T, D), BF16),
        ((T, D), BF16),
        ((2, T), F32),
        ((1, CS, FF), BF16),
        ((1, CS, FF), BF16),
        ((1, CS, FF), BF16),
    )
    outs = tuple(shape(*kind) for kind in kinds)
    parts = pl.pallas_call(
        kernel,
        out_shape=outs,
        in_specs=[vmem, vmem, vmem, vmem, hbm, hbm, hbm],
        out_specs=(hbm,) * 6,
        scratch_shapes=[
            pltpu.VMEM((D, FF), BF16),
            pltpu.VMEM((D, FF), BF16),
            pltpu.VMEM((D, FF), BF16),
            pltpu.VMEM((4, ROWS, W), BF16),
            pltpu.VMEM((4, ROWS, W), BF16),
            pltpu.VMEM((ROWS, D), BF16),
            pltpu.VMEM((ROWS, D), BF16),
            pltpu.VMEM((ROWS, FF), F32),
            pltpu.VMEM((ROWS, FF), F32),
            pltpu.VMEM((ROWS, FF), BF16),
            pltpu.VMEM((ROWS, FF), BF16),
            pltpu.VMEM((ROWS, FF), BF16),
            pltpu.VMEM((4, CS, 3 * FF), BF16),
            pltpu.VMEM((4, CS, 3 * FF), BF16),
            pltpu.VMEM((3, CS, 3 * FF), BF16),
            pltpu.VMEM((HALF, 3 * FF), BF16),
            pltpu.VMEM((HALF, 3 * FF), BF16),
            pltpu.VMEM((CS, 3 * FF), BF16),
            pltpu.VMEM((CS, 3 * FF), BF16),
            *[pltpu.VMEM(*kind) for kind in kinds],
            pltpu.VMEM((3, 8, T), F32),
            pltpu.VMEM((2, 2, T, D), BF16),
            pltpu.VMEM((2, T, D), F32),
            pltpu.VMEM((2, 2, T, D), BF16),
            pltpu.VMEM((2, 2, T, D), BF16),
            pltpu.VMEM((2, 8, T), F32),
            pltpu.VMEM((2, 8, T), F32),
            pltpu.SemaphoreType.DMA((3,)),
            pltpu.SemaphoreType.DMA((4,)),
            pltpu.SemaphoreType.DMA((4,)),
            pltpu.SemaphoreType.DMA((4,)),
            pltpu.SemaphoreType.DMA((4,)),
            pltpu.SemaphoreType.DMA((6,)),
            pltpu.SemaphoreType.DMA((6,)),
            pltpu.SemaphoreType.DMA((6,)),
            pltpu.SemaphoreType.DMA((2, 2)),
            pltpu.SemaphoreType.DMA((2, 2)),
            pltpu.SemaphoreType.DMA((2,)),
            pltpu.SemaphoreType.DMA((2,)),
            pltpu.SemaphoreType.DMA((2, 2)),
            pltpu.SemaphoreType.DMA((2, 2)),
            pltpu.SemaphoreType.DMA((2,)),
            pltpu.SemaphoreType.DMA((2,)),
        ],
        compiler_params=pltpu.CompilerParams(
            collective_id=0, has_side_effects=True, vmem_limit_bytes=64 << 20
        ),
        name="expert_step",
    )(hits, cotangent, combine.T, expert_ids.T, gate_weight, up_weight, down_weight)
    mixed, igrad, cgrad, gate, up, down = pl.pallas_call(
        results,
        out_shape=outs,
        in_specs=[hbm] * 6,
        out_specs=(hbm,) * 6,
        scratch_shapes=[*[pltpu.VMEM(*kind) for kind in kinds], pltpu.SemaphoreType.DMA((2, 6))],
        name="results",
    )(*parts)
    return mixed, igrad, cgrad.T, gate, up, down


def solution(mesh):
    rows = P(("ctx", "exp"), None)
    placed = (rows, rows, rows, rows, P("exp", None, None), P("exp", None, None), P("exp", None, None))
    outs = (rows, rows, rows, P("exp", "ctx", None), P("exp", "ctx", None), P("exp", "ctx", None))
    return jax.shard_map(local, mesh=mesh, in_specs=placed, out_specs=outs, check_vma=False)
```

```python
import functools

import jax
import jax.numpy as jnp
from jax import lax
from jax.experimental import pallas as pl
from jax.experimental.pallas import tpu as pltpu
from jax.sharding import PartitionSpec as P

MESH = pl.DeviceIdType.MESH
F32 = jnp.float32
BF16 = jnp.bfloat16

grad_scale = 0.0625
NZ, NX, NY = 8, 4, 4
EXPERTS = NZ * NX
CAP = 12
T = 128
D = 2048
FF = 768
RB = 16
Q = 512
W = 3 * Q
ROWS = EXPERTS * RB
CS = D // 8
HALF = CS // 2
DYS = (2, 1, 3, 0)


GROUPS = ((0, 64), (64, 288), (288, 512))
WINDOWS = ((0, 128), (32, 256), (256, 256))
SAME = (0, 4, 28)


def hops_of():
    table = {}
    for dz in range(NZ):
        for dx in range(NX):
            i = dz * NX + dx
            if dz == 0:
                table[i] = (0, dx)
            elif i * RB < GROUPS[1][1]:
                table[i] = (dz - 1, dx)
            else:
                table[i] = (dz - NZ + 1, dx)
    order = []
    for pair in ((2, 6), (3, 5), (4, 4), (1, 7), (0, 0)):
        for dx in (0, 1, 2, 3) if pair[0] != pair[1] else (0, 2, 1, 3):
            for dz in sorted(set(pair)):
                order.append(dz * NX + dx)
    return [(i,) + table[i] for i in order if i not in SAME]


def nn(a, b):
    return jnp.dot(a, b, preferred_element_type=F32)


def nt(a, b):
    return lax.dot_general(a, b, (((1,), (1,)), ((), ())), preferred_element_type=F32)


def tn(a, b):
    return lax.dot_general(a, b, (((0,), (0,)), ((), ())), preferred_element_type=F32)


def iota(shape, dim):
    return lax.broadcasted_iota(jnp.int32, shape, dim)


def bits(cond):
    return jnp.where(cond, 1.0, 0.0).astype(BF16)


def kernel(
    hits, cotangent, combine, expert_ids, wg_hbm, wu_hbm, wd_hbm,
    mixed_out, igrad_out, cgrad_out, gate_out, up_out, down_out,
    wg, wu, wd, send, recv, xs, cs, act, fac, hid, gg, gu,
    po, pr, st, ra, rb, r1, r3,
    mixed, igrad, cgrad, gate, up, down,
    metas, raw, own, part_to, part_from, cg_to, cg_from,
    w_sem, send_sem, recv_sem, po_sem, pr_sem, y_send, y_recv, out_sem,
    raw_send, raw_recv, meta_send, meta_recv, part_send, part_recv, cg_send, cg_recv,
):
    c = lax.axis_index("ctx")
    me = lax.axis_index("exp")
    z, x = me // NX, me % NX
    y, core = c // 2, c % 2
    sibling = y * 2 + 1 - core
    y_next = ((y + 1) % NY) * 2 + core
    y_prev = ((y + NY - 1) % NY) * 2 + core
    order = hops_of()

    def peer(dz, dx):
        return ((z + dz + NZ) % NZ) * NX + (x + dx + NX) % NX

    def remote(src, dst, ssem, rsem, ctx, exp):
        return pltpu.make_async_remote_copy(
            src_ref=src, dst_ref=dst, send_sem=ssem, recv_sem=rsem, device_id=(ctx, exp), device_id_type=MESH
        )

    loads = []
    for i, (src, dst) in enumerate(((wg_hbm, wg), (wu_hbm, wu), (wd_hbm, wd))):
        copy = pltpu.make_async_copy(src.at[0], dst, w_sem.at[i])
        copy.start()
        loads.append(copy)

    barrier = pltpu.get_barrier_semaphore()
    near = [(dz, dx) for dz in range(-3, 4) for dx in range(NX) if (dz, dx) != (0, 0)]
    for dz, dx in near:
        pl.semaphore_signal(barrier, inc=1, device_id=(c, peer(dz, dx)), device_id_type=MESH)
    for other in (sibling, y_next, y_prev):
        pl.semaphore_signal(barrier, inc=1, device_id=(other, me), device_id_type=MESH)

    sides = ((peer(1, 0), peer(-1, 0)), (peer(-1, 0), peer(1, 0)))
    metas_sent = [
        remote(metas.at[0], metas.at[1 + i], meta_send.at[i], meta_recv.at[i], c, sides[i][0]) for i in range(2)
    ]
    raw_sent = [
        [remote(src, raw.at[p, i], raw_send.at[p, i], raw_recv.at[p, i], c, sides[i][0]) for i in range(2)]
        for p, src in enumerate((hits, cotangent))
    ]
    parts_sent = [
        [
            remote(part_to.at[p, i], part_from.at[p, i], part_send.at[p, i], part_recv.at[p, i], c, sides[i][1])
            for i in range(2)
        ]
        for p in range(2)
    ]
    cg_sent = [remote(cg_to.at[i], cg_from.at[i], cg_send.at[i], cg_recv.at[i], c, sides[i][1]) for i in range(2)]

    pl.semaphore_wait(barrier, len(near) + 3)
    for i in range(2):
        raw_sent[0][i].start()

    name = iota((EXPERTS, T), 0)
    ids = [expert_ids[k : k + 1, :] for k in range(2)]
    named = bits((name == ids[0]) | (name == ids[1]))
    earlier = bits(iota((T, T), 0) < iota((T, T), 1))
    before = nn(named, earlier)
    slots, tails = [], []
    for k in range(2):
        rank = jnp.sum(jnp.where(name == ids[k], before, 0.0), axis=0, keepdims=True).astype(jnp.int32)
        block = (((ids[k] >> 2) - z) & (NZ - 1)) * NX + (((ids[k] & (NX - 1)) - x) & (NX - 1))
        slots.append(block * RB + rank)
        tails.append((rank >> 2) * ROWS + block * RB + CAP + (rank & 3))
    metas[0] = jnp.concatenate(
        [r.astype(F32) for r in slots + tails] + [combine[0:1, :], combine[1:2, :], jnp.zeros((2, T), F32)],
        axis=0,
    )

    def rows_of(g):
        meta = metas[g]
        return (
            [meta[k : k + 1, :].astype(jnp.int32) for k in range(2)],
            [meta[2 + k : 3 + k, :].astype(jnp.int32) for k in range(2)],
        )

    def columns_of(g):
        turned = jnp.transpose(jnp.concatenate([metas[g]] * (T // 8), axis=0))
        return (
            [turned[:, k : k + 1].astype(jnp.int32) for k in range(2)],
            [turned[:, 2 + k : 3 + k].astype(jnp.int32) for k in range(2)],
            [turned[:, 4 + k : 5 + k] for k in range(2)],
        )

    def copies(phase, back, blocks):
        for i, dz, dx in order:
            if i in blocks:
                to = peer(-dz, -dx) if back else peer(dz, dx)
                part = pl.ds(RB * i, RB)
                remote(
                    send.at[phase, part], recv.at[phase, part], send_sem.at[phase], recv_sem.at[phase], c, to
                ).start()
        for i in SAME:
            if i in blocks:
                recv[phase, RB * i : RB * i + RB, :] = send[phase, RB * i : RB * i + RB, :]

    def whole(phase):
        part = pl.ds(0, RB * len(order))
        return remote(
            send.at[phase, part], recv.at[phase, part], send_sem.at[phase], recv_sem.at[phase], c, peer(1, 0)
        )

    near_blocks = range(0, GROUPS[0][1] // RB)
    far_blocks = range(GROUPS[1][0] // RB, EXPERTS)

    def pack_hits(g, src):
        lo, hi = GROUPS[g]
        s_row, v_row = rows_of(g)
        rows = iota((hi - lo, T), 0) + lo
        d_any = bits((rows == s_row[0]) | (rows == s_row[1]))
        for b in range(3):
            t_any = bits((rows + ROWS * b == v_row[0]) | (rows + ROWS * b == v_row[1]))
            left = jnp.concatenate([d_any, t_any], axis=1)
            right = jnp.concatenate([src[:, Q * b : Q * b + Q], src[:, W:]], axis=0)
            send[0, lo:hi, Q * b : Q * b + Q] = nn(left, right).astype(BF16)

    def pack_cots(g, src):
        lo, hi = GROUPS[g]
        s_row, v_row = rows_of(g)
        weights = columns_of(g)[2]
        rows = iota((hi - lo, T), 0) + lo
        for b in range(3):
            left, right = [], []
            for k in range(2):
                left.append(bits(rows == s_row[k]))
                right.append((weights[k] * src[:, Q * b : Q * b + Q].astype(F32)).astype(BF16))
                left.append(bits(rows + ROWS * b == v_row[k]))
                right.append((weights[k] * src[:, W:].astype(F32)).astype(BF16))
            send[1, lo:hi, Q * b : Q * b + Q] = nn(
                jnp.concatenate(left, axis=1), jnp.concatenate(right, axis=0)
            ).astype(BF16)

    left_over = []

    def leave(i, src, dst):
        copy = pltpu.make_async_copy(src, dst, out_sem.at[i])
        copy.start()
        left_over.append(copy)

    for i in range(2):
        metas_sent[i].start()
    pack_hits(0, hits)
    copies(0, False, near_blocks)
    pack_cots(0, cotangent)

    for i in range(2):
        metas_sent[i].wait_recv()
        raw_sent[0][i].wait_recv()
        if i == 0:
            raw_sent[1][0].start()
            raw_sent[1][1].start()
        pack_hits(1 + i, raw.at[0, i])
    copies(0, False, far_blocks)

    for i in range(2):
        raw_sent[1][i].wait_recv()
        pack_cots(1 + i, raw.at[1, i])
    whole(0).wait_send()
    copies(1, False, range(EXPERTS))

    row = iota((256, 256), 0)
    col = iota((256, 256), 1)
    same = (row >> 4) == (col >> 4)
    keep = jnp.where((iota((256, 1), 0) & 15) < CAP, 1.0, 0.0)
    keep_all = jnp.where((iota((ROWS, 1), 0) & 15) < CAP, 1.0, 0.0)

    def unpack(src, dst):
        for h in range(ROWS // 256):
            part = pl.ds(256 * h, 256)
            tail = jnp.zeros((256, Q), F32)
            for b in range(3):
                block = src[part, Q * b : Q * b + Q]
                dst[part, Q * b : Q * b + Q] = (block.astype(F32) * keep).astype(BF16)
                pick = bits(
                    same & ((row & 15) < CAP) & (((row & 15) >> 2) == b) & ((col & 15) == CAP + (row & 3))
                )
                tail = tail + nn(pick, block)
            dst[part, W:] = tail.astype(BF16)

    def pack(product, dst):
        tail = product(3).astype(BF16)
        for b in range(3):
            main = product(b) * keep_all
            pick = bits(same & ((row & 15) >= CAP) & ((col & 15) == 4 * b + (row & 15) - CAP))
            for h in range(ROWS // 256):
                dst[256 * h : 256 * h + 256, Q * b : Q * b + Q] = (
                    main[256 * h : 256 * h + 256] + nn(pick, tail[256 * h : 256 * h + 256])
                ).astype(BF16)

    whole(0).wait_recv()
    unpack(recv.at[0], xs)
    loads[0].wait()
    loads[1].wait()

    @pl.loop(0, FF // 256)
    def _(n):
        part = pl.ds(pl.multiple_of(n * 256, 256), 256)
        gates = nn(xs[...], wg[:, part])
        ups = nn(xs[...], wu[:, part])
        sig = jax.nn.sigmoid(gates)
        active = gates * sig
        act[:, part] = active
        fac[:, part] = ups * sig * (1.0 + gates * (1.0 - sig))
        hid[:, part] = (active * ups).astype(BF16)

    loads[2].wait()
    pack(lambda b: nt(hid[...], wd[Q * b : Q * b + Q, :]), send.at[2])
    copies(2, True, range(EXPERTS))
    whole(1).wait_send()

    whole(1).wait_recv()
    unpack(recv.at[1], cs)

    @pl.loop(0, FF // 256)
    def _(n):
        part = pl.ds(pl.multiple_of(n * 256, 256), 256)
        grad_hidden = nn(cs[...], wd[:, part])
        gu[:, part] = (grad_hidden * act[:, part]).astype(BF16)
        gg[:, part] = (grad_hidden * fac[:, part]).astype(BF16)

    def weight_terms(owner):
        part = pl.ds(pl.multiple_of(owner * CS, CS), CS)
        return (
            tn(xs[:, part], gg[...]),
            tn(xs[:, part], gu[...]),
            tn(cs[:, part], hid[...]),
        )

    pack(
        lambda b: nt(gg[...], wg[Q * b : Q * b + Q, :]) + nt(gu[...], wu[Q * b : Q * b + Q, :]),
        send.at[3],
    )

    copies(3, True, range(EXPERTS))

    over = []
    for j, dy in enumerate(DYS):
        terms = weight_terms(((y + dy) % NY) * 2 + 1 - core)
        for i in range(3):
            po[j, :, FF * i : FF * i + FF] = terms[i].astype(BF16)
        copy = remote(po.at[j], pr.at[j], po_sem.at[j], pr_sem.at[j], sibling, me)
        copy.start()
        over.append(copy)

    def along(i, src, dst, to):
        return remote(src, dst, y_send.at[i], y_recv.at[i], to, me)

    top, low = pl.ds(0, HALF), pl.ds(HALF, HALF)
    hops = [
        along(0, st.at[0, top], ra, y_next),
        along(1, st.at[0, low], rb, y_prev),
        along(2, st.at[1, low], r1.at[low], y_next),
        along(3, st.at[2, top], r3.at[top], y_prev),
        along(4, st.at[1, top], r1.at[top], y_next),
        along(5, st.at[2, low], r3.at[low], y_prev),
    ]
    for j, dy in enumerate(DYS[:3]):
        terms = weight_terms(((y + dy) % NY) * 2 + core)
        over[j].wait_recv()
        for i in range(3):
            part = slice(FF * i, FF * i + FF)
            st[j, :, part] = (terms[i] + pr[j, :, part].astype(F32)).astype(BF16)
        if j == 0:
            hops[0].start()
            hops[1].start()
        else:
            hops[1 + j].start()

    def picks(g):
        lo, hi = GROUPS[g]
        start, length = WINDOWS[g]
        s_col, v_col, weights = columns_of(g)
        lanes = iota((T, length), 1) + start
        s_pick, v_pick = [], []
        for k in range(2):
            inside = (s_col[k] >= lo) & (s_col[k] < hi)
            s_in = jnp.where(inside, s_col[k], -1)
            v_in = jnp.where(inside, v_col[k], -1)
            s_pick.append(lanes == s_in)
            v_pick.append([lanes + ROWS * b == v_in for b in range(3)])
        return s_pick, v_pick, weights

    whole(2).wait_recv()
    for g in (1, 2, 0):
        s_pick, v_pick, weights = picks(g)
        window = pl.ds(*WINDOWS[g])
        source = cotangent if g == 0 else raw.at[1, g - 1]
        sums = [jnp.zeros((T, 1), F32) for _ in range(2)]
        for b in range(4):
            total = jnp.zeros((T, Q), F32)
            cot = source[:, Q * b : Q * b + Q].astype(F32)
            for k in range(2):
                if b < 3:
                    rows = nn(bits(s_pick[k]), recv[2, window, Q * b : Q * b + Q])
                else:
                    rows = nn(bits(v_pick[k][0]), recv[2, window, 0:Q])
                    rows = rows + nn(bits(v_pick[k][1]), recv[2, window, Q : 2 * Q])
                    rows = rows + nn(bits(v_pick[k][2]), recv[2, window, 2 * Q : W])
                total = total + weights[k] * rows
                sums[k] = sums[k] + jnp.sum(cot * rows, axis=1, keepdims=True)
            if g == 0:
                own[0, :, Q * b : Q * b + Q] = total
            else:
                part_to[0, g - 1, :, Q * b : Q * b + Q] = total.astype(BF16)
        pair = jnp.transpose(jnp.where(iota((T, 128), 1) == 0, sums[0], sums[1]))[0:8, :]
        if g == 0:
            own_pair = pair
        else:
            cg_to[g - 1] = pair

    hops[0].wait_recv()
    st[1, top, :] = (st[1, top, :].astype(F32) + ra[...].astype(F32)).astype(BF16)
    hops[4].start()
    hops[1].wait_recv()
    st[2, low, :] = (st[2, low, :].astype(F32) + rb[...].astype(F32)).astype(BF16)
    hops[5].start()

    whole(2).wait_send()
    whole(3).wait_send()
    for i in range(2):
        parts_sent[0][i].start()
        cg_sent[i].start()

    whole(3).wait_recv()
    for g in (1, 2, 0):
        s_pick, v_pick, _ = picks(g)
        window = pl.ds(*WINDOWS[g])
        s_both = bits(s_pick[0] | s_pick[1])
        v_both = [bits(v_pick[0][b] | v_pick[1][b]) for b in range(3)]
        for b in range(4):
            if b < 3:
                total = nn(s_both, recv[3, window, Q * b : Q * b + Q])
            else:
                total = nn(v_both[0], recv[3, window, 0:Q])
                total = total + nn(v_both[1], recv[3, window, Q : 2 * Q])
                total = total + nn(v_both[2], recv[3, window, 2 * Q : W])
            if g == 0:
                own[1, :, Q * b : Q * b + Q] = total
            else:
                part_to[1, g - 1, :, Q * b : Q * b + Q] = total.astype(BF16)
        if g > 0:
            parts_sent[1][g - 1].start()

    for i in range(2):
        parts_sent[0][i].wait_recv()
        cg_sent[i].wait_recv()
    mixed[...] = (own[0] + part_from[0, 0].astype(F32) + part_from[0, 1].astype(F32)).astype(BF16)
    leave(0, mixed, mixed_out)
    cgrad[...] = (own_pair + cg_from[0] + cg_from[1])[0:2, :]
    leave(1, cgrad, cgrad_out)

    terms = weight_terms(c)
    over[3].wait_recv()
    for i in (2, 3, 4, 5):
        hops[i].wait_recv()
    for i, (out, dst) in enumerate(((gate, gate_out), (up, up_out), (down, down_out))):
        part = slice(FF * i, FF * i + FF)
        total = terms[i] + pr[3, :, part].astype(F32) + r1[:, part].astype(F32) + r3[:, part].astype(F32)
        out[0] = (total * grad_scale).astype(BF16)
        leave(2 + i, out, dst)

    for i in range(2):
        parts_sent[1][i].wait_recv()
    igrad[...] = (own[1] + part_from[1, 0].astype(F32) + part_from[1, 1].astype(F32)).astype(BF16)
    leave(5, igrad, igrad_out)

    for copy in over + hops + metas_sent + cg_sent + sum(raw_sent + parts_sent, []):
        copy.wait_send()
    for copy in left_over:
        copy.wait()


def results(*refs):
    ins, outs, held, sem = refs[:6], refs[6:12], refs[12:18], refs[18]
    inward = [pltpu.make_async_copy(ins[i], held[i], sem.at[0, i]) for i in range(6)]
    outward = [pltpu.make_async_copy(held[i], outs[i], sem.at[1, i]) for i in range(6)]
    for copy in inward:
        copy.start()
    for before, after in zip(inward, outward):
        before.wait()
        after.start()
    for copy in outward:
        copy.wait()


def local(hits, cotangent, combine, expert_ids, gate_weight, up_weight, down_weight):
    vmem = pl.BlockSpec(memory_space=pltpu.VMEM)
    hbm = pl.BlockSpec(memory_space=pl.ANY)
    shape = jax.ShapeDtypeStruct
    kinds = (
        ((T, D), BF16),
        ((T, D), BF16),
        ((2, T), F32),
        ((1, CS, FF), BF16),
        ((1, CS, FF), BF16),
        ((1, CS, FF), BF16),
    )
    outs = tuple(shape(*kind) for kind in kinds)
    parts = pl.pallas_call(
        kernel,
        out_shape=outs,
        in_specs=[vmem, vmem, vmem, vmem, hbm, hbm, hbm],
        out_specs=(hbm,) * 6,
        scratch_shapes=[
            pltpu.VMEM((D, FF), BF16),
            pltpu.VMEM((D, FF), BF16),
            pltpu.VMEM((D, FF), BF16),
            pltpu.VMEM((4, ROWS, W), BF16),
            pltpu.VMEM((4, ROWS, W), BF16),
            pltpu.VMEM((ROWS, D), BF16),
            pltpu.VMEM((ROWS, D), BF16),
            pltpu.VMEM((ROWS, FF), F32),
            pltpu.VMEM((ROWS, FF), F32),
            pltpu.VMEM((ROWS, FF), BF16),
            pltpu.VMEM((ROWS, FF), BF16),
            pltpu.VMEM((ROWS, FF), BF16),
            pltpu.VMEM((4, CS, 3 * FF), BF16),
            pltpu.VMEM((4, CS, 3 * FF), BF16),
            pltpu.VMEM((3, CS, 3 * FF), BF16),
            pltpu.VMEM((HALF, 3 * FF), BF16),
            pltpu.VMEM((HALF, 3 * FF), BF16),
            pltpu.VMEM((CS, 3 * FF), BF16),
            pltpu.VMEM((CS, 3 * FF), BF16),
            *[pltpu.VMEM(*kind) for kind in kinds],
            pltpu.VMEM((3, 8, T), F32),
            pltpu.VMEM((2, 2, T, D), BF16),
            pltpu.VMEM((2, T, D), F32),
            pltpu.VMEM((2, 2, T, D), BF16),
            pltpu.VMEM((2, 2, T, D), BF16),
            pltpu.VMEM((2, 8, T), F32),
            pltpu.VMEM((2, 8, T), F32),
            pltpu.SemaphoreType.DMA((3,)),
            pltpu.SemaphoreType.DMA((4,)),
            pltpu.SemaphoreType.DMA((4,)),
            pltpu.SemaphoreType.DMA((4,)),
            pltpu.SemaphoreType.DMA((4,)),
            pltpu.SemaphoreType.DMA((6,)),
            pltpu.SemaphoreType.DMA((6,)),
            pltpu.SemaphoreType.DMA((6,)),
            pltpu.SemaphoreType.DMA((2, 2)),
            pltpu.SemaphoreType.DMA((2, 2)),
            pltpu.SemaphoreType.DMA((2,)),
            pltpu.SemaphoreType.DMA((2,)),
            pltpu.SemaphoreType.DMA((2, 2)),
            pltpu.SemaphoreType.DMA((2, 2)),
            pltpu.SemaphoreType.DMA((2,)),
            pltpu.SemaphoreType.DMA((2,)),
        ],
        compiler_params=pltpu.CompilerParams(
            collective_id=0, has_side_effects=True, vmem_limit_bytes=64 << 20
        ),
        name="expert_step",
    )(hits, cotangent, combine.T, expert_ids.T, gate_weight, up_weight, down_weight)
    mixed, igrad, cgrad, gate, up, down = pl.pallas_call(
        results,
        out_shape=outs,
        in_specs=[hbm] * 6,
        out_specs=(hbm,) * 6,
        scratch_shapes=[*[pltpu.VMEM(*kind) for kind in kinds], pltpu.SemaphoreType.DMA((2, 6))],
        name="results",
    )(*parts)
    return mixed, igrad, cgrad.T, gate, up, down


def solution(mesh):
    rows = P(("ctx", "exp"), None)
    placed = (rows, rows, rows, rows, P("exp", None, None), P("exp", None, None), P("exp", None, None))
    outs = (rows, rows, rows, P("exp", "ctx", None), P("exp", "ctx", None), P("exp", "ctx", None))
    return jax.shard_map(local, mesh=mesh, in_specs=placed, out_specs=outs, check_vma=False)
```
